256 devices in a mesh: atoms: 32 (over z, x), aux: 8 (over y, core).
Axes of the slice: x: 4, y: 4, z: 8, core: 2. Of those that a mesh axis runs over, the one named last changes fastest.
Arguments:
- factors: bfloat16 [32, 48, 512, 512], P('atoms', 'aux'), may hold values from -0.25 to 0.25
- density: bfloat16 [32, 2, 512, 512], P('atoms'), may hold values from -2 to 2
- screen: int32 [32, 2], P('atoms'), may hold values from 0 to 1, as said below
Outputs:
- exchange: float32 [32, 4, 512, 512], P('atoms', None, 'aux')
The draws below stay inside these ranges and needn't reach their ends.
Inputs may be any that keep to these rules, and one draw needn't show every extreme that they name: `screen`: entry [a, o] is 1 where the pair of atom blocks a and a + o + 1 survives screening and 0 where a + o + 1 >= 32; atom block 2 keeps all its pairs with blocks 0 to 4.
All inputs are finite; a program needn't handle non-finite values.
Results may differ from the reference program's by a relative error of at most 0.0029.
Values may be sent and summed in bfloat16 or wider, within the bound.
No kernel may reach another device: no remote copies, remote signals or barrier semaphores. Data moves between devices by JAX's collectives and lax.ppermute only.
A program may use at most 64 MiB of HBM per device.

```python
import jax
import jax.numpy as jnp
from jax import lax

BASIS = 512
REACH = 2
BLOCKS = 32
AUX_ALL = 48


def draw_screen(key, part):
    kept = (jax.random.randint(key, (BLOCKS, REACH), 0, 4) > 0).astype(jnp.int32)
    block_ids = jnp.arange(BLOCKS, dtype=jnp.int32)[:, None]
    offsets = jnp.arange(REACH, dtype=jnp.int32)[None, :] + 1
    forced = (block_ids == 2) | (block_ids + offsets == 2)
    kept = jnp.where(forced, 1, kept)
    return jnp.where(block_ids + offsets < BLOCKS, kept, 0).astype(jnp.int32)


def levels(rng, shape, shards, smallest, largest):
    gain = 1.0
    for position, blocks in shards:
        draws = jax.random.uniform(jax.random.fold_in(jax.random.fold_in(rng, 6), position), (blocks,), jnp.float32, smallest / len(shards), largest / len(shards))
        gain = gain * jnp.repeat(jnp.exp(draws), shape[position] // blocks).reshape((-1,) + (1,) * (len(shape) - 1 - position))
    return gain


def gaussian(rng, extent, scale, most, pieces=(), held_as=jnp.bfloat16):
    level = levels(rng, extent, pieces, -0.22, 0.18) if pieces else 1.0
    entries = jax.random.normal(rng, extent, jnp.float32) * scale * level
    return jnp.minimum(jnp.maximum(entries, -most), most).astype(held_as)


def setup_inputs(seed: int = 0) -> dict:
    splits = jax.random.split(jax.random.key(seed), 4)
    factors = gaussian(splits[0], (BLOCKS, AUX_ALL, BASIS, BASIS), BASIS ** -0.5, 0.25, ((0, 32), (1, 8)))
    density = gaussian(splits[1], (BLOCKS, REACH, BASIS, BASIS), (AUX_ALL ** -0.5), 2.0, ((0, 32),))
    screen = draw_screen(jax.random.fold_in(splits[3], 71), 0)
    return {"factors": factors, "density": density, "screen": screen}


def pair_block(first_factor, second_factor, density_block):
    width = density_block.shape[0]
    transformed = jnp.dot(first_factor.reshape(-1, width), density_block, preferred_element_type=jnp.float32)
    transformed = transformed.astype(jnp.bfloat16).reshape(first_factor.shape)
    return lax.dot_general(transformed.astype(jnp.float32), second_factor.astype(jnp.float32), (((0, 2), (0, 2)), ((), ())))


def reference(factors, density, screen):
    def one_block(index):
        owned = factors[index]
        results = []
        for offset in range(1, REACH + 1):
            partner = factors[jnp.minimum(index + offset, BLOCKS - 1)]
            contribution = pair_block(owned, partner, density[index, offset - 1])
            results.append(contribution * screen[index, offset - 1].astype(jnp.float32))
        return jnp.stack(results)

    upper = lax.map(one_block, jnp.arange(BLOCKS, dtype=jnp.int32))
    lowers = []
    for offset in range(1, REACH + 1):
        moved = jnp.concatenate([jnp.zeros((offset, BASIS, BASIS), jnp.float32), upper[:BLOCKS - offset, offset - 1]], axis=0)
        lowers.append(jnp.swapaxes(moved, 1, 2))
    uppers = [upper[:, offset] for offset in range(REACH)]
    return jnp.stack(uppers + lowers, axis=1)
```

```python
import jax
import jax.numpy as jnp
from jax import lax
from jax.sharding import PartitionSpec as P

CHUNKS = 3


def shift(value, axis, steps, wrap):
    count = lax.axis_size(axis)
    pairs = [(i, (i + steps) % count) for i in range(count) if wrap or 0 <= i + steps < count]
    return lax.ppermute(value, axis, pairs)


def swap_core(value):
    return lax.ppermute(value, "aux", [(i, i ^ 1) for i in range(lax.axis_size("aux"))])


def shift_y(value, steps):
    count = lax.axis_size("aux")
    return lax.ppermute(value, "aux", [(i, (i + 2 * steps) % count) for i in range(count)])


def transform(owned, density_block, flag):
    out = jnp.einsum("pmk,kl->pml", owned, density_block, preferred_element_type=jnp.float32)
    return out.astype(jnp.bfloat16) * flag.astype(jnp.bfloat16)


def contract(left, right):
    return lax.dot_general(left, right, (((0, 2), (0, 2)), ((), ())), preferred_element_type=jnp.float32)


def body(factors, density, screen):
    owned = factors[0]
    count, width = owned.shape[0], owned.shape[1]
    per = count // CHUNKS
    rows = width // lax.axis_size("aux")
    far = transform(owned, density[0, 1], screen[0, 1])
    near = transform(owned, density[0, 0], screen[0, 0])
    first, second = 0.0, 0.0
    for index in range(CHUNKS):
        part = slice(index * per, (index + 1) * per)
        ahead = shift(owned[part], "atoms", -1, False)
        behind = shift(far[part], "atoms", 1, False)
        first = first + contract(near[part], ahead)
        second = second + contract(behind, ahead)
    position = lax.axis_index("aux")
    core, place = position % 2, position // 2
    blocks = jnp.stack([first, second, first.T, second.T]).reshape(4, 4, 2, rows, width)
    kept = lax.dynamic_index_in_dim(blocks, core, 2, keepdims=False)
    sent = lax.dynamic_index_in_dim(blocks, 1 - core, 2, keepdims=False).astype(jnp.bfloat16)
    kept = kept + swap_core(sent).astype(jnp.float32)
    total = lax.dynamic_index_in_dim(kept, place, 1, keepdims=False)
    narrow = kept.astype(jnp.bfloat16)
    for steps in (2, 1, 3):
        piece = lax.dynamic_index_in_dim(narrow, (place + steps) % 4, 1, keepdims=False)
        total = total + shift_y(piece, steps).astype(jnp.float32)
    narrow = total.astype(jnp.bfloat16)
    upper_far = shift(narrow[1], "atoms", -1, False).astype(jnp.float32)
    lower = shift(narrow[2:], "atoms", 1, False).astype(jnp.float32)
    return jnp.concatenate([total[:1], upper_far[None], lower])[None]


def solution(mesh):
    in_specs = (P("atoms", "aux", None, None), P("atoms", None, None, None), P("atoms", None))
    out_specs = P("atoms", None, "aux", None)
    return jax.shard_map(body, mesh=mesh, in_specs=in_specs, out_specs=out_specs, check_vma=False)
```

```python
import jax
import jax.numpy as jnp
from jax import lax
from jax.experimental import pallas as pl
from jax.experimental.pallas import tpu as pltpu
from jax.sharding import PartitionSpec as P

CHUNKS = 3
F32, BF16 = jnp.float32, jnp.bfloat16
VMEM = pl.BlockSpec(memory_space=pltpu.VMEM)
SMEM = pl.BlockSpec(memory_space=pltpu.SMEM)


def params(limit=24):
    return pltpu.CompilerParams(vmem_limit_bytes=limit * 1024 * 1024)


def shift(value, axis, steps):
    count = lax.axis_size(axis)
    return lax.ppermute(value, axis, [(i, i + steps) for i in range(count) if 0 <= i + steps < count])


def swap_core(value):
    return lax.ppermute(value, "aux", [(i, i ^ 1) for i in range(lax.axis_size("aux"))])


def shift_y(value, steps):
    count = lax.axis_size("aux")
    return lax.ppermute(value, "aux", [(i, (i + 2 * steps) % count) for i in range(count)])


def transform(owned, density, screen, which, start, size):
    width = owned.shape[-1]

    def kernel(flag, left, right, out):
        product = jnp.dot(left[0], right[0], preferred_element_type=F32).astype(BF16)
        out[0] = product * flag[0, which].astype(F32).astype(BF16)

    return pl.pallas_call(
        kernel,
        grid=(size,),
        in_specs=[
            SMEM,
            pl.BlockSpec((1, width, width), lambda i: (start + i, 0, 0)),
            pl.BlockSpec((1, width, width), lambda i: (which, 0, 0)),
        ],
        out_specs=pl.BlockSpec((1, width, width), lambda i: (i, 0, 0)),
        out_shape=jax.ShapeDtypeStruct((size, width, width), BF16),
        compiler_params=params(),
        cost_estimate=pl.CostEstimate(
            flops=2 * size * width**3, bytes_accessed=4 * size * width**2, transcendentals=0
        ),
    )(screen, owned, density)


def contract(left, right):
    return lax.dot_general(left, right, (((0, 2), (0, 2)), ((), ())), preferred_element_type=F32)


def finish(place, first, second, near, behind, ahead, rows):
    size, width = near.shape[0], near.shape[1]
    places = width // (2 * rows)

    def kernel(place, first, second, near, behind, ahead, kept, sent, scratch):
        core = place[0]
        for index, (start, left) in enumerate(((first, near), (second, behind))):
            total = start[...]
            for step in range(size):
                total = total + lax.dot_general(
                    left[step], ahead[step], (((1,), (1,)), ((), ())), preferred_element_type=F32
                )
            scratch[index] = total
            scratch[2 + index] = total.T
        for block in range(4):
            for y in range(places):
                own = pl.ds(pl.multiple_of(2 * y * rows + core * rows, rows), rows)
                other = pl.ds(pl.multiple_of(2 * y * rows + (1 - core) * rows, rows), rows)
                sent[block, y] = scratch[block, other, :].astype(BF16)
                kept[block, y] = scratch[block, own, :]

    shape = (4, places, rows, width)
    return pl.pallas_call(
        kernel,
        in_specs=[SMEM] + [VMEM] * 5,
        out_specs=[VMEM, VMEM],
        out_shape=[jax.ShapeDtypeStruct(shape, F32), jax.ShapeDtypeStruct(shape, BF16)],
        scratch_shapes=[pltpu.VMEM((4, width, width), F32)],
        compiler_params=params(),
        cost_estimate=pl.CostEstimate(
            flops=4 * size * width**3, bytes_accessed=14 * width**2, transcendentals=0
        ),
    )(place, first, second, near, behind, ahead)


def join_core(place, kept, received):
    blocks, places, rows, width = kept.shape

    def kernel(place, kept, received, total, *pieces):
        y = place[1]
        total[...] = kept[:, y] + received[:, y].astype(F32)
        for steps in range(1, places):
            target = lax.rem(y + steps, places)
            pieces[steps - 1][...] = (kept[:, target] + received[:, target].astype(F32)).astype(BF16)

    shape = (blocks, rows, width)
    return pl.pallas_call(
        kernel,
        in_specs=[SMEM, VMEM, VMEM],
        out_specs=[VMEM] * places,
        out_shape=[jax.ShapeDtypeStruct(shape, F32)] + [jax.ShapeDtypeStruct(shape, BF16)] * (places - 1),
        compiler_params=params(),
        cost_estimate=pl.CostEstimate(flops=kept.size, bytes_accessed=8 * kept.size, transcendentals=0),
    )(place, kept, received)


def join_places(total, received):
    _, rows, width = total.shape

    def kernel(total, one, two, three, upper, upper_far, lower):
        value = total[...] + one[...].astype(F32) + two[...].astype(F32) + three[...].astype(F32)
        upper[...] = value[0]
        upper_far[...] = value[1].astype(BF16)
        lower[...] = value[2:].astype(BF16)

    return pl.pallas_call(
        kernel,
        in_specs=[VMEM] * 4,
        out_specs=[VMEM] * 3,
        out_shape=[
            jax.ShapeDtypeStruct((rows, width), F32),
            jax.ShapeDtypeStruct((rows, width), BF16),
            jax.ShapeDtypeStruct((2, rows, width), BF16),
        ],
        compiler_params=params(),
        cost_estimate=pl.CostEstimate(flops=total.size * 3, bytes_accessed=12 * total.size, transcendentals=0),
    )(total, *received)


def assemble(upper, upper_far, lower):
    rows, width = upper.shape

    def kernel(upper, upper_far, lower, out):
        out[0, 0] = upper[...]
        out[0, 1] = upper_far[...].astype(F32)
        out[0, 2:] = lower[...].astype(F32)

    return pl.pallas_call(
        kernel,
        in_specs=[VMEM] * 3,
        out_specs=VMEM,
        out_shape=jax.ShapeDtypeStruct((1, 4, rows, width), F32),
        compiler_params=params(),
    )(upper, upper_far, lower)


def body(factors, density, screen):
    owned, blocks = factors[0], density[0]
    count, width = owned.shape[0], owned.shape[1]
    per = count // CHUNKS
    position = lax.axis_index("aux")
    place = jnp.stack([position % 2, position // 2]).astype(jnp.int32)
    ahead, behind = [], []
    for index in range(CHUNKS):
        piece = owned[index * per : (index + 1) * per]
        piece, owned = lax.optimization_barrier((piece, owned))
        ahead.append(shift(piece, "atoms", -1))
        behind.append(shift(transform(owned, blocks, screen, 1, index * per, per), "atoms", 1))
    near = transform(owned, blocks, screen, 0, 0, count)
    first, second = 0.0, 0.0
    for index in range(CHUNKS - 1):
        first = first + contract(near[index * per : (index + 1) * per], ahead[index])
        second = second + contract(behind[index], ahead[index])
    rows = width // lax.axis_size("aux")
    kept, sent = finish(place, first, second, near[count - per :], behind[-1], ahead[-1], rows)
    total, *pieces = join_core(place, kept, swap_core(sent))
    received = [shift_y(piece, steps) for steps, piece in enumerate(pieces, 1)]
    upper, upper_far, lower = join_places(total, received)
    return assemble(upper, shift(upper_far, "atoms", -1), shift(lower, "atoms", 1))


def solution(mesh):
    in_specs = (P("atoms", "aux", None, None), P("atoms", None, None, None), P("atoms", None))
    out_specs = P("atoms", None, "aux", None)
    return jax.shard_map(body, mesh=mesh, in_specs=in_specs, out_specs=out_specs, check_vma=False)
```

```python
import jax
import jax.numpy as jnp
from jax import lax
from jax.experimental import pallas as pl
from jax.experimental.pallas import tpu as pltpu
from jax.sharding import PartitionSpec as P


F32, BF16 = jnp.float32, jnp.bfloat16
VMEM = pl.BlockSpec(memory_space=pltpu.VMEM)
SMEM = pl.BlockSpec(memory_space=pltpu.SMEM)
LANES = 128
ROWS, PARTS = 64, 8
CHUNKS = ((0, 16), (32, 32), (16, 16))
EARLY, LATE = 384, 128
EARLY_U1, EARLY_U2, EARLY_ALL = 192, 144, 672
LATE_U1, LATE_U2, LATE_ALL = 64, 112, 352


def params(limit=20):
    return pltpu.CompilerParams(vmem_limit_bytes=limit * 1024 * 1024)


def cost(flops, size):
    return pl.CostEstimate(flops=flops, bytes_accessed=size, transcendentals=0)


def shift(value, axis, steps):
    count = lax.axis_size(axis)
    return lax.ppermute(value, axis, [(i, i + steps) for i in range(count) if 0 <= i + steps < count])


def swap_core(value):
    return lax.ppermute(value, "aux", [(i, i ^ 1) for i in range(lax.axis_size("aux"))])


def shift_y(value, steps):
    count = lax.axis_size("aux")
    return lax.ppermute(value, "aux", [(i, (i + 2 * steps) % count) for i in range(count)])


def split(factors, density, screen, start, size):
    count, width = factors.shape[0], factors.shape[-1]
    height = PARTS * size

    def kernel(flag, left, right, piece, far):
        value = left[0].reshape(height, width)
        piece[...] = value
        product = jnp.dot(value, right[0], preferred_element_type=F32).astype(BF16)
        far[...] = product * flag[0, 1].astype(F32).astype(BF16)

    return pl.pallas_call(
        kernel,
        grid=(count,),
        in_specs=[
            SMEM,
            pl.BlockSpec((1, PARTS, size, width), lambda i: (i, 0, start // size, 0)),
            pl.BlockSpec((1, width, width), lambda i: (1, 0, 0)),
        ],
        out_specs=[pl.BlockSpec((height, width), lambda i: (0, i))] * 2,
        out_shape=[jax.ShapeDtypeStruct((height, count * width), BF16)] * 2,
        cost_estimate=cost(2 * height * count * width**2, 6 * height * count * width),
    )(screen, factors, density)


def transform(factors, density, screen):
    count, width = factors.shape[0], factors.shape[-1]

    def kernel(flag, left, right, out):
        product = jnp.dot(left[0].reshape(width, width), right[0], preferred_element_type=F32).astype(BF16)
        out[...] = product * flag[0, 0].astype(F32).astype(BF16)

    return pl.pallas_call(
        kernel,
        grid=(count,),
        in_specs=[
            SMEM,
            pl.BlockSpec((1, PARTS, ROWS, width), lambda i: (i, 0, 0, 0)),
            pl.BlockSpec((1, width, width), lambda i: (0, 0, 0)),
        ],
        out_specs=pl.BlockSpec((width, width), lambda i: (0, i)),
        out_shape=jax.ShapeDtypeStruct((width, count * width), BF16),
        compiler_params=params(),
        cost_estimate=cost(2 * count * width**3, 4 * count * width**2),
    )(screen, factors, density)


def contract(left, right):
    return lax.dot_general(left, right, (((1,), (1,)), ((), ())), preferred_element_type=F32)


def early_rows(ref, part, columns):
    low = ref[pl.ds(pl.multiple_of(16 * part, 16), 16), columns]
    high = ref[pl.ds(pl.multiple_of(128 + 32 * part, 32), 32), columns]
    return low, high


def late_rows(ref, part, columns):
    return ref[pl.ds(pl.multiple_of(16 * part, 16), 16), columns]


def put(out, y, offset, values):
    for value in values:
        out[y, pl.ds(offset, value.shape[0]), :] = value.astype(out.dtype)
        offset += value.shape[0]
    return offset


def lanes(index):
    return pl.ds(index * LANES, LANES)


def pack_early(place, near, ahead, behind):
    width = near.shape[0]
    places = PARTS // 2

    def kernel(place, near, ahead0, ahead1, behind0, behind1, kept, sent, upper, lower, upper_far, lower_far):
        offset = 0
        for right in (ahead0, ahead1):
            columns = pl.ds(offset, right.shape[0])
            value = contract(near[...], right[...])
            upper[:, columns] = value
            lower[columns, :] = value.T
            row = 0
            for left in (behind0, behind1):
                value = contract(left[...], right[...])
                upper_far[pl.ds(row, left.shape[0]), columns] = value
                lower_far[columns, pl.ds(row, left.shape[0])] = value.T
                row += left.shape[0]
            offset += right.shape[0]
        for y in range(places):
            for out, core in ((sent, 1 - place[0]), (kept, place[0])):
                part = 2 * y + core
                own = pl.ds(pl.multiple_of(ROWS * part, ROWS), ROWS)
                at = put(out, y, 0, [upper[own, lanes(t)] for t in range(3)])
                for t in range(3):
                    at = put(out, y, at, early_rows(upper_far, part, lanes(t)))
                for t in range(4):
                    at = put(out, y, at, early_rows(lower, part, lanes(t)))
                for t in range(3):
                    at = put(out, y, at, early_rows(lower_far, part, lanes(t)))

    shape = (places, EARLY_ALL, LANES)
    return pl.pallas_call(
        kernel,
        in_specs=[SMEM] + [VMEM] * 5,
        out_specs=[VMEM] * 2,
        out_shape=[jax.ShapeDtypeStruct(shape, F32), jax.ShapeDtypeStruct(shape, BF16)],
        scratch_shapes=[
            pltpu.VMEM((width, EARLY), F32),
            pltpu.VMEM((EARLY, width), F32),
            pltpu.VMEM((EARLY, EARLY), F32),
            pltpu.VMEM((EARLY, EARLY), F32),
        ],
        compiler_params=params(),
        cost_estimate=cost(2 * near.size * EARLY * 2, near.size * 4),
    )(place, near, *ahead, *behind)


def pack_late(place, near, ahead, behind):
    width = near.shape[0]
    places = PARTS // 2

    def kernel(place, near, ahead0, ahead1, ahead2, behind0, behind1, behind2, kept, sent, upper, lower, tall, wide, tall_t, wide_t):
        value = contract(near[...], ahead2[...])
        upper[...] = value
        lower[...] = value.T
        offset = 0
        for left, right in ((behind0, ahead0), (behind1, ahead1)):
            span = pl.ds(offset, left.shape[0])
            value = contract(left[...], ahead2[...])
            tall[span, :] = value
            wide_t[:, span] = value.T
            value = contract(behind2[...], right[...])
            wide[:, span] = value
            tall_t[span, :] = value.T
            offset += left.shape[0]
        value = contract(behind2[...], ahead2[...])
        wide[:, pl.ds(EARLY, LATE)] = value
        wide_t[:, pl.ds(EARLY, LATE)] = value.T
        for y in range(places):
            for out, core in ((sent, 1 - place[0]), (kept, place[0])):
                part = 2 * y + core
                own = pl.ds(pl.multiple_of(ROWS * part, ROWS), ROWS)
                at = put(out, y, 0, [upper[own, :]])
                at = put(out, y, at, early_rows(tall, part, lanes(0)))
                at = put(out, y, at, [late_rows(wide, part, lanes(t)) for t in range(4)])
                at = put(out, y, at, [late_rows(lower, part, lanes(t)) for t in range(4)])
                at = put(out, y, at, early_rows(tall_t, part, lanes(0)))
                at = put(out, y, at, [late_rows(wide_t, part, lanes(t)) for t in range(4)])

    shape = (places, LATE_ALL, LANES)
    return pl.pallas_call(
        kernel,
        in_specs=[SMEM] + [VMEM] * 7,
        out_specs=[VMEM] * 2,
        out_shape=[jax.ShapeDtypeStruct(shape, F32), jax.ShapeDtypeStruct(shape, BF16)],
        scratch_shapes=[
            pltpu.VMEM((width, LATE), F32),
            pltpu.VMEM((LATE, width), F32),
            pltpu.VMEM((EARLY, LATE), F32),
            pltpu.VMEM((LATE, width), F32),
            pltpu.VMEM((EARLY, LATE), F32),
            pltpu.VMEM((LATE, width), F32),
        ],
        compiler_params=params(),
        cost_estimate=cost(2 * near.size * LATE * 3, near.size * 6),
    )(place, near, *ahead, *behind)


def join_core(place, kept, received):
    places, rows, width = kept.shape

    def kernel(place, kept, received, total, *pieces):
        y = place[1]
        total[...] = kept[y] + received[y].astype(F32)
        for steps in range(1, places):
            target = lax.rem(y + steps, places)
            pieces[steps - 1][...] = (kept[target] + received[target].astype(F32)).astype(BF16)

    shape = (rows, width)
    return pl.pallas_call(
        kernel,
        in_specs=[SMEM, VMEM, VMEM],
        out_specs=[VMEM] * places,
        out_shape=[jax.ShapeDtypeStruct(shape, F32)] + [jax.ShapeDtypeStruct(shape, BF16)] * (places - 1),
        compiler_params=params(),
        cost_estimate=cost(kept.size, 8 * kept.size),
    )(place, kept, received)


def join_places(total, received, first, second):
    rows, width = total.shape
    sizes = (first, second, rows - first - second)

    def kernel(total, one, two, three, *outs):
        offset = 0
        for out, size in zip(outs, sizes):
            span = pl.ds(offset, size)
            value = total[span, :] + one[span, :].astype(F32) + two[span, :].astype(F32) + three[span, :].astype(F32)
            out[...] = value.astype(out.dtype)
            offset += size

    return pl.pallas_call(
        kernel,
        in_specs=[VMEM] * 4,
        out_specs=[VMEM] * 3,
        out_shape=[jax.ShapeDtypeStruct((size, width), dtype) for size, dtype in zip(sizes, (F32, BF16, BF16))],
        compiler_params=params(),
        cost_estimate=cost(total.size * 3, 12 * total.size),
    )(total, *received)


def after(value, *others):
    return lax.optimization_barrier((value, *others))[0]


def send_places(pieces):
    received = []
    for steps in (2, 1, 3):
        received.append(shift_y(pieces[steps - 1], steps))
    return received


def hop(upper, upper_far, lower):
    return upper, shift(upper_far, "atoms", -1), shift(lower, "atoms", 1)


def assemble(order, early, late):
    width = order.shape[0]

    def far(early, late, base, late_base):
        chunks = []
        blocks = [early[pl.ds(base + 48 * t, 48), :] for t in range(3)]
        blocks.append(late[pl.ds(late_base, 48), :])
        body = jnp.concatenate(blocks, axis=1)
        last = jnp.concatenate([late[pl.ds(late_base + 48 + 16 * t, 16), :] for t in range(4)], axis=1)
        chunks = [body[:16], last, body[16:]]
        return jnp.concatenate(chunks, axis=0)

    def kernel(order, upper0, far0, lower0, upper1, far1, lower1, out):
        exact = order[...]
        blocks = [upper0[pl.ds(ROWS * t, ROWS), :] for t in range(3)] + [upper1[...]]
        value = jnp.concatenate(blocks, axis=1)
        out[0, 0] = jnp.dot(value, exact.astype(F32), preferred_element_type=F32, precision=lax.Precision.HIGHEST)
        out[0, 1] = jnp.dot(far(far0, far1, 0, 0), exact, preferred_element_type=F32)
        for t in range(4):
            out[0, 2, pl.ds(0, 16), lanes(t)] = lower0[pl.ds(48 * t, 16), :].astype(F32)
            out[0, 2, pl.ds(16, 16), lanes(t)] = lower1[pl.ds(16 * t, 16), :].astype(F32)
            out[0, 2, pl.ds(32, 32), lanes(t)] = lower0[pl.ds(48 * t + 16, 32), :].astype(F32)
        out[0, 3] = jnp.dot(far(lower0, lower1, 192, 64), exact, preferred_element_type=F32)

    return pl.pallas_call(
        kernel,
        in_specs=[VMEM] * 7,
        out_specs=VMEM,
        out_shape=jax.ShapeDtypeStruct((1, 4, ROWS, width), F32),
        compiler_params=params(),
        cost_estimate=cost(2 * 8 * ROWS * width**2, 4 * ROWS * width * 8),
    )(order, *early, *late)


def natural_order(width):
    index = jnp.arange(width)
    low = ROWS * (index // 16) + index % 16
    high = ROWS * ((index - 128) // 32) + 32 + index % 32
    last = ROWS * ((index - EARLY) // 16) + 16 + index % 16
    place = jnp.where(index < 128, low, jnp.where(index < EARLY, high, last))
    return (place[:, None] == jnp.arange(width)[None, :]).astype(BF16)


def body(factors, density, screen):
    count, width = factors.shape[1], factors.shape[2]
    owned, blocks = factors[0].reshape(count, PARTS, ROWS, width), density[0]
    position = lax.axis_index("aux")
    place = jnp.stack([position % 2, position // 2]).astype(jnp.int32)
    ahead, behind = [], []
    source = owned
    for start, size in CHUNKS:
        piece, far = split(source, blocks, screen, start, size)
        source = after(owned, piece)
        ahead.append(shift(piece, "atoms", -1))
        behind.append(shift(far, "atoms", 1))
    near = transform(source, blocks, screen)
    kept, sent = pack_early(place, near, ahead[:2], behind[:2])
    total, *pieces = join_core(place, kept, swap_core(sent))
    received = send_places(pieces)
    kept, sent = pack_late(after(place, *pieces), near, ahead, behind)
    late_total, *late_pieces = join_core(place, kept, swap_core(sent))
    late_received = send_places(late_pieces)
    early = hop(*join_places(after(total, *late_pieces), received, EARLY_U1, EARLY_U2))
    late = hop(*join_places(late_total, late_received, LATE_U1, LATE_U2))
    return assemble(natural_order(width), early, late)


def solution(mesh):
    in_specs = (P("atoms", "aux", None, None), P("atoms", None, None, None), P("atoms", None))
    out_specs = P("atoms", None, "aux", None)
    return jax.shard_map(body, mesh=mesh, in_specs=in_specs, out_specs=out_specs, check_vma=False)
```

```python
import jax
import jax.numpy as jnp
from jax import lax
from jax.experimental import pallas as pl
from jax.experimental.pallas import tpu as pltpu
from jax.sharding import PartitionSpec as P


F32, BF16 = jnp.float32, jnp.bfloat16
VMEM = pl.BlockSpec(memory_space=pltpu.VMEM)
SMEM = pl.BlockSpec(memory_space=pltpu.SMEM)
LANES = 128
ROWS, PARTS, STEP = 64, 8, 3
CHUNKS = ((0, 16), (32, 32), (16, 16))
EARLY, LATE = 384, 128
EARLY_U1, EARLY_U2, EARLY_ALL = 192, 144, 672
LATE_U1, LATE_U2, LATE_ALL = 64, 112, 352


def params(limit=20):
    return pltpu.CompilerParams(vmem_limit_bytes=limit * 1024 * 1024)


def cost(flops, size):
    return pl.CostEstimate(flops=flops, bytes_accessed=size, transcendentals=0)


def swap_atoms(value, first):
    count = lax.axis_size("atoms")
    pairs = [(i, i + 1) for i in range(first, count - 1, 2)]
    return lax.ppermute(value, "atoms", pairs + [(j, i) for i, j in pairs])


def swap_core(value):
    return lax.ppermute(value, "aux", [(i, i ^ 1) for i in range(lax.axis_size("aux"))])


def shift_y(value, steps):
    count = lax.axis_size("aux")
    return lax.ppermute(value, "aux", [(i, (i + 2 * steps) % count) for i in range(count)])


def split(place, factors, density, screen, start, size):
    count, width = factors.shape[0], factors.shape[-1]
    height = PARTS * size

    def kernel(place, flag, left, right, first, second):
        scale = flag[0, 1].astype(F32).astype(BF16)
        even = place[2] == 0
        for step in range(STEP):
            columns = pl.ds(step * width, width)
            piece = left[step].reshape(height, width)
            far = jnp.dot(piece, right[0], preferred_element_type=F32).astype(BF16) * scale
            first[:, columns] = jnp.where(even, far, piece)
            second[:, columns] = jnp.where(even, piece, far)

    return pl.pallas_call(
        kernel,
        grid=(count // STEP,),
        in_specs=[
            SMEM,
            SMEM,
            pl.BlockSpec((STEP, PARTS, size, width), lambda i: (i, 0, start // size, 0)),
            pl.BlockSpec((1, width, width), lambda i: (1, 0, 0)),
        ],
        out_specs=[pl.BlockSpec((height, STEP * width), lambda i: (0, i))] * 2,
        out_shape=[jax.ShapeDtypeStruct((height, count * width), BF16)] * 2,
        cost_estimate=cost(2 * height * count * width**2, 6 * height * count * width),
    )(place, screen, factors, density)


def transform(factors, density, screen):
    count, width = factors.shape[0], factors.shape[-1]

    def kernel(flag, left, right, out):
        scale = flag[0, 0].astype(F32).astype(BF16)
        for step in range(STEP):
            piece = left[step].reshape(width, width)
            product = jnp.dot(piece, right[0], preferred_element_type=F32).astype(BF16)
            out[:, pl.ds(step * width, width)] = product * scale

    return pl.pallas_call(
        kernel,
        grid=(count // STEP,),
        in_specs=[
            SMEM,
            pl.BlockSpec((STEP, PARTS, ROWS, width), lambda i: (i, 0, 0, 0)),
            pl.BlockSpec((1, width, width), lambda i: (0, 0, 0)),
        ],
        out_specs=pl.BlockSpec((width, STEP * width), lambda i: (0, i)),
        out_shape=jax.ShapeDtypeStruct((width, count * width), BF16),
        compiler_params=params(),
        cost_estimate=cost(2 * count * width**3, 4 * count * width**2),
    )(screen, factors, density)


def contract(left, right):
    return lax.dot_general(left, right, (((1,), (1,)), ((), ())), preferred_element_type=F32)


def early_rows(ref, part, columns):
    low = ref[pl.ds(pl.multiple_of(16 * part, 16), 16), columns]
    high = ref[pl.ds(pl.multiple_of(128 + 32 * part, 32), 32), columns]
    return low, high


def late_rows(ref, part, columns):
    return ref[pl.ds(pl.multiple_of(16 * part, 16), 16), columns]


def put(out, y, offset, values):
    for value in values:
        out[y, pl.ds(offset, value.shape[0]), :] = value.astype(out.dtype)
        offset += value.shape[0]
    return offset


def lanes(index):
    return pl.ds(index * LANES, LANES)


def pick(place, first, second):
    even = place[2] == 0
    first, second = first[...], second[...]
    return jnp.where(even, first, second), jnp.where(even, second, first)


def pack_early(place, near, first, second):
    width, depth = near.shape
    places = PARTS // 2

    def kernel(place, near, first0, second0, first1, second1, kept, sent, ahead, behind, upper, lower, upper_far, lower_far):
        low, high = pl.ds(0, 128), pl.ds(128, 256)
        ahead[low, :], behind[low, :] = pick(place, first0, second0)
        ahead[high, :], behind[high, :] = pick(place, first1, second1)
        value = contract(near[...], ahead[...])
        upper[...] = value
        lower[...] = value.T
        value = contract(behind[...], ahead[...])
        upper_far[...] = value
        lower_far[...] = value.T
        for y in range(places):
            for out, core in ((sent, 1 - place[0]), (kept, place[0])):
                part = 2 * y + core
                own = pl.ds(pl.multiple_of(ROWS * part, ROWS), ROWS)
                at = put(out, y, 0, [upper[own, lanes(t)] for t in range(3)])
                for t in range(3):
                    at = put(out, y, at, early_rows(upper_far, part, lanes(t)))
                for t in range(4):
                    at = put(out, y, at, early_rows(lower, part, lanes(t)))
                for t in range(3):
                    at = put(out, y, at, early_rows(lower_far, part, lanes(t)))

    shape = (places, EARLY_ALL, LANES)
    return pl.pallas_call(
        kernel,
        in_specs=[SMEM] + [VMEM] * 5,
        out_specs=[VMEM] * 4,
        out_shape=[
            jax.ShapeDtypeStruct(shape, F32),
            jax.ShapeDtypeStruct(shape, BF16),
            jax.ShapeDtypeStruct((EARLY, depth), BF16),
            jax.ShapeDtypeStruct((EARLY, depth), BF16),
        ],
        scratch_shapes=[
            pltpu.VMEM((width, EARLY), F32),
            pltpu.VMEM((EARLY, width), F32),
            pltpu.VMEM((EARLY, EARLY), F32),
            pltpu.VMEM((EARLY, EARLY), F32),
        ],
        compiler_params=params(),
        cost_estimate=cost(2 * near.size * EARLY * 2, near.size * 4),
    )(place, near, first[0], second[0], first[1], second[1])


def pack_late(place, near, ahead, behind, first, second):
    width = near.shape[0]
    places = PARTS // 2

    def kernel(place, near, ahead, behind, first, second, kept, sent, upper, lower, tall, wide, tall_t, wide_t):
        last, prior = pick(place, first, second)
        value = contract(near[...], last)
        upper[...] = value
        lower[...] = value.T
        value = contract(behind[...], last)
        tall[...] = value
        wide_t[:, pl.ds(0, EARLY)] = value.T
        value = contract(ahead[...], prior)
        tall_t[...] = value
        wide[:, pl.ds(0, EARLY)] = value.T
        value = contract(prior, last)
        wide[:, pl.ds(EARLY, LATE)] = value
        wide_t[:, pl.ds(EARLY, LATE)] = value.T
        for y in range(places):
            for out, core in ((sent, 1 - place[0]), (kept, place[0])):
                part = 2 * y + core
                own = pl.ds(pl.multiple_of(ROWS * part, ROWS), ROWS)
                at = put(out, y, 0, [upper[own, :]])
                at = put(out, y, at, early_rows(tall, part, lanes(0)))
                at = put(out, y, at, [late_rows(wide, part, lanes(t)) for t in range(4)])
                at = put(out, y, at, [late_rows(lower, part, lanes(t)) for t in range(4)])
                at = put(out, y, at, early_rows(tall_t, part, lanes(0)))
                at = put(out, y, at, [late_rows(wide_t, part, lanes(t)) for t in range(4)])

    shape = (places, LATE_ALL, LANES)
    return pl.pallas_call(
        kernel,
        in_specs=[SMEM] + [VMEM] * 5,
        out_specs=[VMEM] * 2,
        out_shape=[jax.ShapeDtypeStruct(shape, F32), jax.ShapeDtypeStruct(shape, BF16)],
        scratch_shapes=[
            pltpu.VMEM((width, LATE), F32),
            pltpu.VMEM((LATE, width), F32),
            pltpu.VMEM((EARLY, LATE), F32),
            pltpu.VMEM((LATE, width), F32),
            pltpu.VMEM((EARLY, LATE), F32),
            pltpu.VMEM((LATE, width), F32),
        ],
        compiler_params=params(),
        cost_estimate=cost(2 * near.size * LATE * 3, near.size * 6),
    )(place, near, ahead, behind, first, second)


def join_core(place, kept, received):
    places, rows, width = kept.shape

    def kernel(place, kept, received, total, *pieces):
        y = place[1]
        total[...] = kept[y] + received[y].astype(F32)
        for steps in range(1, places):
            target = lax.rem(y + steps, places)
            pieces[steps - 1][...] = (kept[target] + received[target].astype(F32)).astype(BF16)

    shape = (rows, width)
    return pl.pallas_call(
        kernel,
        in_specs=[SMEM, VMEM, VMEM],
        out_specs=[VMEM] * places,
        out_shape=[jax.ShapeDtypeStruct(shape, F32)] + [jax.ShapeDtypeStruct(shape, BF16)] * (places - 1),
        compiler_params=params(),
        cost_estimate=cost(kept.size, 8 * kept.size),
    )(place, kept, received)


def after(value, *others):
    return lax.optimization_barrier((value, *others))[0]


def send_places(pieces):
    received = []
    for steps in (2, 1, 3):
        received.append(shift_y(pieces[steps - 1], steps))
    return received


def gather(refs, span):
    total, *received = refs
    value = total[span, :]
    for piece in received:
        value = value + piece[span, :].astype(F32)
    return value


def join_early(total, received):
    rows, width = total.shape

    def kernel(total, one, two, three, upper, rest):
        refs = (total, one, two, three)
        upper[...] = gather(refs, pl.ds(0, EARLY_U1))
        rest[...] = gather(refs, pl.ds(EARLY_U1, rows - EARLY_U1)).astype(BF16)

    return pl.pallas_call(
        kernel,
        in_specs=[VMEM] * 4,
        out_specs=[VMEM] * 2,
        out_shape=[
            jax.ShapeDtypeStruct((EARLY_U1, width), F32),
            jax.ShapeDtypeStruct((rows - EARLY_U1, width), BF16),
        ],
        compiler_params=params(),
        cost_estimate=cost(total.size * 3, 12 * total.size),
    )(total, *received)


def join_late(place, rest, total, received):
    rows, width = total.shape
    far = EARLY_U2 + LATE_U2
    low = rest.shape[0] - EARLY_U2
    height = low + rows - LATE_U1 - LATE_U2

    def kernel(place, rest, total, one, two, three, upper, first, second):
        refs = (total, one, two, three)
        even = place[2] == 0
        upper[...] = gather(refs, pl.ds(0, LATE_U1))
        late_far = gather(refs, pl.ds(LATE_U1, LATE_U2)).astype(BF16)
        late_low = gather(refs, pl.ds(LATE_U1 + LATE_U2, rows - LATE_U1 - LATE_U2)).astype(BF16)

        def write(lower, upper_far):
            lower[pl.ds(0, low), :] = rest[pl.ds(EARLY_U2, low), :]
            lower[pl.ds(low, late_low.shape[0]), :] = late_low
            upper_far[pl.ds(0, EARLY_U2), :] = rest[pl.ds(0, EARLY_U2), :]
            upper_far[pl.ds(EARLY_U2, LATE_U2), :] = late_far
            upper_far[pl.ds(far, height - far), :] = jnp.zeros((height - far, width), BF16)

        pl.when(even)(lambda: write(first, second))
        pl.when(jnp.logical_not(even))(lambda: write(second, first))

    return pl.pallas_call(
        kernel,
        in_specs=[SMEM] + [VMEM] * 5,
        out_specs=[VMEM] * 3,
        out_shape=[
            jax.ShapeDtypeStruct((LATE_U1, width), F32),
            jax.ShapeDtypeStruct((height, width), BF16),
            jax.ShapeDtypeStruct((height, width), BF16),
        ],
        compiler_params=params(),
        cost_estimate=cost(total.size * 3, 12 * total.size),
    )(place, rest, total, *received)


def restore(order, early, late):
    width = order.shape[0]

    def kernel(order, early, late, out):
        blocks = [early[pl.ds(ROWS * t, ROWS), :] for t in range(3)] + [late[...]]
        value = jnp.concatenate(blocks, axis=1)
        exact = order[...].astype(F32)
        out[...] = jnp.dot(value, exact, preferred_element_type=F32, precision=lax.Precision.HIGHEST)

    return pl.pallas_call(
        kernel,
        in_specs=[VMEM] * 3,
        out_specs=VMEM,
        out_shape=jax.ShapeDtypeStruct((ROWS, width), F32),
        compiler_params=params(),
        cost_estimate=cost(2 * 6 * ROWS * width**2, 4 * width**2),
    )(order, early, late)


def assemble(place, order, upper, first, second):
    width = order.shape[0]
    late_low = 3 * 144 - 96

    def rows(ref, base, late):
        body = jnp.concatenate(
            [ref[pl.ds(base + 48 * t, 48), :] for t in range(3)] + [ref[pl.ds(late, 48), :]], axis=1
        )
        last = jnp.concatenate([ref[pl.ds(late + 48 + 16 * t, 16), :] for t in range(4)], axis=1)
        return jnp.concatenate([body[:16], last, body[16:]], axis=0)

    def kernel(place, order, upper, first, second, out):
        out[0, 0] = upper[...]

        def write(far, low):
            exact = order[...]
            out[0, 1] = jnp.dot(rows(far, 0, EARLY_U2), exact, preferred_element_type=F32)
            for t in range(4):
                out[0, 2, pl.ds(0, 16), lanes(t)] = low[pl.ds(48 * t, 16), :].astype(F32)
                out[0, 2, pl.ds(16, 16), lanes(t)] = low[pl.ds(late_low + 16 * t, 16), :].astype(F32)
                out[0, 2, pl.ds(32, 32), lanes(t)] = low[pl.ds(48 * t + 16, 32), :].astype(F32)
            out[0, 3] = jnp.dot(rows(low, 192, late_low + 64), exact, preferred_element_type=F32)

        pl.when(place[2] == 0)(lambda: write(first, second))
        pl.when(place[2] != 0)(lambda: write(second, first))

    return pl.pallas_call(
        kernel,
        in_specs=[SMEM] + [VMEM] * 4,
        out_specs=VMEM,
        out_shape=jax.ShapeDtypeStruct((1, 4, ROWS, width), F32),
        compiler_params=params(),
        cost_estimate=cost(2 * 2 * ROWS * width**2, 4 * ROWS * width * 8),
    )(place, order, upper, first, second)


def natural_order(width):
    index = jnp.arange(width)
    low = ROWS * (index // 16) + index % 16
    high = ROWS * ((index - 128) // 32) + 32 + index % 32
    last = ROWS * ((index - EARLY) // 16) + 16 + index % 16
    place = jnp.where(index < 128, low, jnp.where(index < EARLY, high, last))
    return (place[:, None] == jnp.arange(width)[None, :]).astype(BF16)


def body(factors, density, screen):
    count, width = factors.shape[1], factors.shape[2]
    owned, blocks = factors[0].reshape(count, PARTS, ROWS, width), density[0]
    position = lax.axis_index("aux")
    place = jnp.stack([position % 2, position // 2, lax.axis_index("atoms") % 2]).astype(jnp.int32)
    first, second = [], []
    source = owned
    for start, size in CHUNKS:
        one, two = split(place, source, blocks, screen, start, size)
        source = after(owned, one)
        first.append(swap_atoms(one, 0))
        second.append(swap_atoms(two, 1))
    near = transform(source, blocks, screen)
    kept, sent, ahead, behind = pack_early(place, near, first[:2], second[:2])
    total, *pieces = join_core(place, kept, swap_core(sent))
    received = send_places(pieces)
    kept, sent = pack_late(after(place, *pieces), near, ahead, behind, first[2], second[2])
    late_total, *late_pieces = join_core(place, kept, swap_core(sent))
    late_received = send_places(late_pieces)
    upper, rest = join_early(after(total, *late_pieces), received)
    late_upper, one, two = join_late(place, rest, late_total, late_received)
    one = swap_atoms(one, 0)
    two = swap_atoms(two, 1)
    order = natural_order(width)
    upper = restore(order, upper, late_upper)
    return assemble(place, order, upper, one, two)


def solution(mesh):
    in_specs = (P("atoms", "aux", None, None), P("atoms", None, None, None), P("atoms", None))
    out_specs = P("atoms", None, "aux", None)
    return jax.shard_map(body, mesh=mesh, in_specs=in_specs, out_specs=out_specs, check_vma=False)
```

```python
import jax
import jax.numpy as jnp
from jax import lax
from jax.experimental import pallas as pl
from jax.experimental.pallas import tpu as pltpu
from jax.sharding import PartitionSpec as P


F32, BF16 = jnp.float32, jnp.bfloat16
VMEM = pl.BlockSpec(memory_space=pltpu.VMEM)
SMEM = pl.BlockSpec(memory_space=pltpu.SMEM)
LANES = 128
ROWS, PARTS, STEP = 64, 8, 3
CHUNKS = ((0, 16, 0, 6), (32, 32, 0, 6), (16, 16, 0, 3), (16, 16, 3, 3))
EARLY, LATE = 384, 128
EARLY_U1, EARLY_U2, EARLY_ALL = 192, 144, 672
LATE_U1, LATE_U2, LATE_ALL = 64, 112, 352


def params(limit=20):
    return pltpu.CompilerParams(vmem_limit_bytes=limit * 1024 * 1024)


def cost(flops, size):
    return pl.CostEstimate(flops=flops, bytes_accessed=size, transcendentals=0)


def swap_atoms(value, first):
    count = lax.axis_size("atoms")
    pairs = [(i, i + 1) for i in range(first, count - 1, 2)]
    return lax.ppermute(value, "atoms", pairs + [(j, i) for i, j in pairs])


def swap_core(value):
    return lax.ppermute(value, "aux", [(i, i ^ 1) for i in range(lax.axis_size("aux"))])


def shift_y(value, steps):
    count = lax.axis_size("aux")
    return lax.ppermute(value, "aux", [(i, (i + 2 * steps) % count) for i in range(count)])


def spot():
    aux = lax.axis_index("aux")
    return lax.rem(aux, 2), lax.div(aux, 2)


def on_even():
    return lax.rem(lax.axis_index("atoms"), 2) == 0


def split(factors, density, screen, start, size, begin, count):
    width = factors.shape[-1]
    height = PARTS * size

    def kernel(flag, left, right, first, second):
        scale = flag[0, 1].astype(F32).astype(BF16)
        even = on_even()
        for step in range(STEP):
            columns = pl.ds(step * width, width)
            piece = left[step].reshape(height, width)
            far = jnp.dot(piece, right[0], preferred_element_type=F32).astype(BF16) * scale
            first[:, columns] = jnp.where(even, far, piece)
            second[:, columns] = jnp.where(even, piece, far)

    return pl.pallas_call(
        kernel,
        grid=(count // STEP,),
        in_specs=[
            SMEM,
            pl.BlockSpec((STEP, PARTS, size, width), lambda i: (begin // STEP + i, 0, start // size, 0)),
            pl.BlockSpec((1, width, width), lambda i: (1, 0, 0)),
        ],
        out_specs=[pl.BlockSpec((height, STEP * width), lambda i: (0, i))] * 2,
        out_shape=[jax.ShapeDtypeStruct((height, count * width), BF16)] * 2,
        cost_estimate=cost(2 * height * count * width**2, 6 * height * count * width),
    )(screen, factors, density)


def transform(factors, density, screen):
    count, width = factors.shape[0], factors.shape[-1]

    def kernel(flag, left, right, out):
        scale = flag[0, 0].astype(F32).astype(BF16)
        for step in range(STEP):
            piece = left[step].reshape(width, width)
            product = jnp.dot(piece, right[0], preferred_element_type=F32).astype(BF16)
            out[:, pl.ds(step * width, width)] = product * scale

    return pl.pallas_call(
        kernel,
        grid=(count // STEP,),
        in_specs=[
            SMEM,
            pl.BlockSpec((STEP, PARTS, ROWS, width), lambda i: (i, 0, 0, 0)),
            pl.BlockSpec((1, width, width), lambda i: (0, 0, 0)),
        ],
        out_specs=pl.BlockSpec((width, STEP * width), lambda i: (0, i)),
        out_shape=jax.ShapeDtypeStruct((width, count * width), BF16),
        compiler_params=params(),
        cost_estimate=cost(2 * count * width**3, 4 * count * width**2),
    )(screen, factors, density)


def contract(left, right):
    return lax.dot_general(left, right, (((1,), (1,)), ((), ())), preferred_element_type=F32)


def early_rows(ref, part, columns):
    low = ref[pl.ds(pl.multiple_of(16 * part, 16), 16), columns]
    high = ref[pl.ds(pl.multiple_of(128 + 32 * part, 32), 32), columns]
    return low, high


def late_rows(ref, part, columns):
    return ref[pl.ds(pl.multiple_of(16 * part, 16), 16), columns]


def put(out, y, offset, values):
    for value in values:
        out[y, pl.ds(offset, value.shape[0]), :] = value.astype(out.dtype)
        offset += value.shape[0]
    return offset


def lanes(index):
    return pl.ds(index * LANES, LANES)


def pick(first, second):
    even = on_even()
    first, second = first[...], second[...]
    return jnp.where(even, first, second), jnp.where(even, second, first)


def pack_early(near, first, second):
    width, depth = near.shape
    places = PARTS // 2

    def kernel(near, first0, second0, first1, second1, kept, sent, ahead, behind, upper, lower, upper_far, lower_far):
        low, high = pl.ds(0, 128), pl.ds(128, 256)
        ahead[low, :], behind[low, :] = pick(first0, second0)
        ahead[high, :], behind[high, :] = pick(first1, second1)
        value = contract(near[...], ahead[...])
        upper[...] = value
        lower[...] = value.T
        value = contract(behind[...], ahead[...])
        upper_far[...] = value
        lower_far[...] = value.T
        mine = spot()[0]
        for y in range(places):
            for out, core in ((sent, 1 - mine), (kept, mine)):
                part = 2 * y + core
                own = pl.ds(pl.multiple_of(ROWS * part, ROWS), ROWS)
                at = put(out, y, 0, [upper[own, lanes(t)] for t in range(3)])
                for t in range(3):
                    at = put(out, y, at, early_rows(upper_far, part, lanes(t)))
                for t in range(4):
                    at = put(out, y, at, early_rows(lower, part, lanes(t)))
                for t in range(3):
                    at = put(out, y, at, early_rows(lower_far, part, lanes(t)))

    shape = (places, EARLY_ALL, LANES)
    return pl.pallas_call(
        kernel,
        in_specs=[VMEM] * 5,
        out_specs=[VMEM] * 4,
        out_shape=[
            jax.ShapeDtypeStruct(shape, F32),
            jax.ShapeDtypeStruct(shape, BF16),
            jax.ShapeDtypeStruct((EARLY, depth), BF16),
            jax.ShapeDtypeStruct((EARLY, depth), BF16),
        ],
        scratch_shapes=[
            pltpu.VMEM((width, EARLY), F32),
            pltpu.VMEM((EARLY, width), F32),
            pltpu.VMEM((EARLY, EARLY), F32),
            pltpu.VMEM((EARLY, EARLY), F32),
        ],
        compiler_params=params(),
        cost_estimate=cost(2 * near.size * EARLY * 2, near.size * 4),
    )(near, first[0], second[0], first[1], second[1])


def pack_middle(near, ahead, behind, first, second):
    width = near.shape[0]
    depth = first.shape[1]

    def kernel(near, ahead, behind, first, second, upper, tall, tall_t, corner):
        last, prior = pick(first, second)
        columns = pl.ds(0, depth)
        upper[...] = contract(near[:, columns], last)
        tall[...] = contract(behind[:, columns], last)
        tall_t[...] = contract(ahead[:, columns], prior)
        corner[...] = contract(prior, last)

    return pl.pallas_call(
        kernel,
        in_specs=[VMEM] * 5,
        out_specs=[VMEM] * 4,
        out_shape=[jax.ShapeDtypeStruct((height, LATE), F32) for height in (width, EARLY, EARLY, LATE)],
        compiler_params=params(),
        cost_estimate=cost(near.size * LATE * 3, near.size * 6),
    )(near, ahead, behind, first, second)


def pack_late(near, ahead, behind, middle, first, second):
    width = near.shape[0]
    places = PARTS // 2
    depth = first.shape[1]

    def kernel(near, ahead, behind, upper0, tall0, tall_t0, corner0, first, second, kept, sent, upper, lower, tall, wide, tall_t, wide_t):
        last, prior = pick(first, second)
        columns = pl.ds(near.shape[1] - depth, depth)
        value = upper0[...] + contract(near[:, columns], last)
        upper[...] = value
        lower[...] = value.T
        value = tall0[...] + contract(behind[:, columns], last)
        tall[...] = value
        wide_t[:, pl.ds(0, EARLY)] = value.T
        value = tall_t0[...] + contract(ahead[:, columns], prior)
        tall_t[...] = value
        wide[:, pl.ds(0, EARLY)] = value.T
        value = corner0[...] + contract(prior, last)
        wide[:, pl.ds(EARLY, LATE)] = value
        wide_t[:, pl.ds(EARLY, LATE)] = value.T
        mine = spot()[0]
        for y in range(places):
            for out, core in ((sent, 1 - mine), (kept, mine)):
                part = 2 * y + core
                own = pl.ds(pl.multiple_of(ROWS * part, ROWS), ROWS)
                at = put(out, y, 0, [upper[own, :]])
                at = put(out, y, at, early_rows(tall, part, lanes(0)))
                at = put(out, y, at, [late_rows(wide, part, lanes(t)) for t in range(4)])
                at = put(out, y, at, [late_rows(lower, part, lanes(t)) for t in range(4)])
                at = put(out, y, at, early_rows(tall_t, part, lanes(0)))
                at = put(out, y, at, [late_rows(wide_t, part, lanes(t)) for t in range(4)])

    shape = (places, LATE_ALL, LANES)
    return pl.pallas_call(
        kernel,
        in_specs=[VMEM] * 9,
        out_specs=[VMEM] * 2,
        out_shape=[jax.ShapeDtypeStruct(shape, F32), jax.ShapeDtypeStruct(shape, BF16)],
        scratch_shapes=[
            pltpu.VMEM((width, LATE), F32),
            pltpu.VMEM((LATE, width), F32),
            pltpu.VMEM((EARLY, LATE), F32),
            pltpu.VMEM((LATE, width), F32),
            pltpu.VMEM((EARLY, LATE), F32),
            pltpu.VMEM((LATE, width), F32),
        ],
        compiler_params=params(),
        cost_estimate=cost(near.size * LATE * 3, near.size * 6),
    )(near, ahead, behind, *middle, first, second)


def join_core(kept, received):
    places, rows, width = kept.shape

    def kernel(kept, received, total, *pieces):
        y = spot()[1]
        total[...] = kept[y] + received[y].astype(F32)
        for steps in range(1, places):
            target = lax.rem(y + steps, places)
            pieces[steps - 1][...] = (kept[target] + received[target].astype(F32)).astype(BF16)

    shape = (rows, width)
    return pl.pallas_call(
        kernel,
        in_specs=[VMEM, VMEM],
        out_specs=[VMEM] * places,
        out_shape=[jax.ShapeDtypeStruct(shape, F32)] + [jax.ShapeDtypeStruct(shape, BF16)] * (places - 1),
        compiler_params=params(),
        cost_estimate=cost(kept.size, 8 * kept.size),
    )(kept, received)


def after(value, *others):
    return lax.optimization_barrier((value, *others))[0]


def send_places(pieces):
    received = []
    for steps in (2, 1, 3):
        received.append(shift_y(pieces[steps - 1], steps))
    return received


def gather(refs, span):
    total, *received = refs
    value = total[span, :]
    for piece in received:
        value = value + piece[span, :].astype(F32)
    return value


def join_early(total, received):
    rows, width = total.shape

    def kernel(total, one, two, three, upper, rest):
        refs = (total, one, two, three)
        upper[...] = gather(refs, pl.ds(0, EARLY_U1))
        rest[...] = gather(refs, pl.ds(EARLY_U1, rows - EARLY_U1)).astype(BF16)

    return pl.pallas_call(
        kernel,
        in_specs=[VMEM] * 4,
        out_specs=[VMEM] * 2,
        out_shape=[
            jax.ShapeDtypeStruct((EARLY_U1, width), F32),
            jax.ShapeDtypeStruct((rows - EARLY_U1, width), BF16),
        ],
        compiler_params=params(),
        cost_estimate=cost(total.size * 3, 12 * total.size),
    )(total, *received)


def join_late(rest, total, received):
    rows, width = total.shape
    far = EARLY_U2 + LATE_U2
    low = rest.shape[0] - EARLY_U2
    height = low + rows - LATE_U1 - LATE_U2

    def kernel(rest, total, one, two, three, upper, first, second):
        refs = (total, one, two, three)
        even = on_even()
        upper[...] = gather(refs, pl.ds(0, LATE_U1))
        late_far = gather(refs, pl.ds(LATE_U1, LATE_U2)).astype(BF16)
        late_low = gather(refs, pl.ds(LATE_U1 + LATE_U2, rows - LATE_U1 - LATE_U2)).astype(BF16)

        def write(lower, upper_far):
            lower[pl.ds(0, low), :] = rest[pl.ds(EARLY_U2, low), :]
            lower[pl.ds(low, late_low.shape[0]), :] = late_low
            upper_far[pl.ds(0, EARLY_U2), :] = rest[pl.ds(0, EARLY_U2), :]
            upper_far[pl.ds(EARLY_U2, LATE_U2), :] = late_far
            upper_far[pl.ds(far, height - far), :] = jnp.zeros((height - far, width), BF16)

        pl.when(even)(lambda: write(first, second))
        pl.when(jnp.logical_not(even))(lambda: write(second, first))

    return pl.pallas_call(
        kernel,
        in_specs=[VMEM] * 5,
        out_specs=[VMEM] * 3,
        out_shape=[
            jax.ShapeDtypeStruct((LATE_U1, width), F32),
            jax.ShapeDtypeStruct((height, width), BF16),
            jax.ShapeDtypeStruct((height, width), BF16),
        ],
        compiler_params=params(),
        cost_estimate=cost(total.size * 3, 12 * total.size),
    )(rest, total, *received)


def restore(order, early, late):
    width = order.shape[0]

    def kernel(order, early, late, out):
        blocks = [early[pl.ds(ROWS * t, ROWS), :] for t in range(3)] + [late[...]]
        value = jnp.concatenate(blocks, axis=1)
        exact = order[...].astype(F32)
        out[...] = jnp.dot(value, exact, preferred_element_type=F32, precision=lax.Precision.HIGHEST)

    return pl.pallas_call(
        kernel,
        in_specs=[VMEM] * 3,
        out_specs=VMEM,
        out_shape=jax.ShapeDtypeStruct((ROWS, width), F32),
        compiler_params=params(),
        cost_estimate=cost(2 * 6 * ROWS * width**2, 4 * width**2),
    )(order, early, late)


def assemble(order, upper, first, second):
    width = order.shape[0]
    late_low = 3 * 144 - 96

    def rows(ref, base, late):
        body = jnp.concatenate(
            [ref[pl.ds(base + 48 * t, 48), :] for t in range(3)] + [ref[pl.ds(late, 48), :]], axis=1
        )
        last = jnp.concatenate([ref[pl.ds(late + 48 + 16 * t, 16), :] for t in range(4)], axis=1)
        return jnp.concatenate([body[:16], last, body[16:]], axis=0)

    def kernel(order, upper, first, second, out):
        even = on_even()
        out[0, 0] = upper[...]

        def write(far, low):
            exact = order[...]
            out[0, 1] = jnp.dot(rows(far, 0, EARLY_U2), exact, preferred_element_type=F32)
            for t in range(4):
                out[0, 2, pl.ds(0, 16), lanes(t)] = low[pl.ds(48 * t, 16), :].astype(F32)
                out[0, 2, pl.ds(16, 16), lanes(t)] = low[pl.ds(late_low + 16 * t, 16), :].astype(F32)
                out[0, 2, pl.ds(32, 32), lanes(t)] = low[pl.ds(48 * t + 16, 32), :].astype(F32)
            out[0, 3] = jnp.dot(rows(low, 192, late_low + 64), exact, preferred_element_type=F32)

        pl.when(even)(lambda: write(first, second))
        pl.when(jnp.logical_not(even))(lambda: write(second, first))

    return pl.pallas_call(
        kernel,
        in_specs=[VMEM] * 4,
        out_specs=VMEM,
        out_shape=jax.ShapeDtypeStruct((1, 4, ROWS, width), F32),
        compiler_params=params(),
        cost_estimate=cost(2 * 2 * ROWS * width**2, 4 * ROWS * width * 8),
    )(order, upper, first, second)


def natural_order(width):
    index = jnp.arange(width)
    low = ROWS * (index // 16) + index % 16
    high = ROWS * ((index - 128) // 32) + 32 + index % 32
    last = ROWS * ((index - EARLY) // 16) + 16 + index % 16
    place = jnp.where(index < 128, low, jnp.where(index < EARLY, high, last))
    return (place[:, None] == jnp.arange(width)[None, :]).astype(BF16)


def body(factors, density, screen):
    count, width = factors.shape[1], factors.shape[2]
    owned, blocks = factors[0].reshape(count, PARTS, ROWS, width), density[0]
    first, second = [], []
    source = owned
    for chunk in CHUNKS:
        one, two = split(source, blocks, screen, *chunk)
        source = after(owned, one)
        second.append(swap_atoms(two, 1))
        first.append(swap_atoms(one, 0))
    near = transform(source, blocks, screen)
    kept, sent, ahead, behind = pack_early(near, first[:2], second[:2])
    total, *pieces = join_core(kept, swap_core(sent))
    received = send_places(pieces)
    middle = pack_middle(near, ahead, behind, first[2], second[2])
    kept, sent = pack_late(near, ahead, behind, middle, first[3], second[3])
    late_total, *late_pieces = join_core(kept, swap_core(sent))
    late_received = send_places(late_pieces)
    upper, rest = join_early(after(total, *late_pieces), received)
    late_upper, one, two = join_late(rest, late_total, late_received)
    two = swap_atoms(two, 1)
    one = swap_atoms(one, 0)
    order = natural_order(width)
    upper = restore(order, upper, late_upper)
    return assemble(order, upper, one, two)


def solution(mesh):
    in_specs = (P("atoms", "aux", None, None), P("atoms", None, None, None), P("atoms", None))
    out_specs = P("atoms", None, "aux", None)
    return jax.shard_map(body, mesh=mesh, in_specs=in_specs, out_specs=out_specs, check_vma=False)
```

```python
import jax
import jax.numpy as jnp
from jax import lax
from jax.experimental import pallas as pl
from jax.experimental.pallas import tpu as pltpu
from jax.sharding import PartitionSpec as P


F32, BF16 = jnp.float32, jnp.bfloat16
VMEM = pl.BlockSpec(memory_space=pltpu.VMEM)
SMEM = pl.BlockSpec(memory_space=pltpu.SMEM)
LANES = 128
ROWS, PARTS, STEP = 64, 8, 3
CHUNKS = ((0, 16, 0, 6), (32, 32, 0, 3), (32, 32, 3, 3), (16, 16, 0, 3), (16, 16, 3, 3))
EARLY, LATE = 384, 128
EARLY_U1, EARLY_U2, EARLY_ALL = 192, 144, 672
LATE_U1, LATE_U2, LATE_ALL = 64, 112, 352


def params(limit=20):
    return pltpu.CompilerParams(vmem_limit_bytes=limit * 1024 * 1024)


def cost(flops, size):
    return pl.CostEstimate(flops=flops, bytes_accessed=size, transcendentals=0)


def swap_atoms(value, first):
    count = lax.axis_size("atoms")
    pairs = [(i, i + 1) for i in range(first, count - 1, 2)]
    return lax.ppermute(value, "atoms", pairs + [(j, i) for i, j in pairs])


def swap_core(value):
    return lax.ppermute(value, "aux", [(i, i ^ 1) for i in range(lax.axis_size("aux"))])


def shift_y(value, steps):
    count = lax.axis_size("aux")
    return lax.ppermute(value, "aux", [(i, (i + 2 * steps) % count) for i in range(count)])


def spot():
    aux = lax.axis_index("aux")
    return lax.rem(aux, 2), lax.div(aux, 2)


def on_even():
    return lax.rem(lax.axis_index("atoms"), 2) == 0


def split(factors, density, screen, start, size, begin, count):
    width = factors.shape[-1]
    height = PARTS * size

    def kernel(flag, left, right, first, second):
        scale = flag[0, 1].astype(F32).astype(BF16)
        even = on_even()
        for step in range(STEP):
            columns = pl.ds(step * width, width)
            piece = left[step].reshape(height, width)
            far = jnp.dot(piece, right[0], preferred_element_type=F32).astype(BF16) * scale
            first[:, columns] = jnp.where(even, far, piece)
            second[:, columns] = jnp.where(even, piece, far)

    return pl.pallas_call(
        kernel,
        grid=(count // STEP,),
        in_specs=[
            SMEM,
            pl.BlockSpec((STEP, PARTS, size, width), lambda i: (begin // STEP + i, 0, start // size, 0)),
            pl.BlockSpec((1, width, width), lambda i: (1, 0, 0)),
        ],
        out_specs=[pl.BlockSpec((height, STEP * width), lambda i: (0, i))] * 2,
        out_shape=[jax.ShapeDtypeStruct((height, count * width), BF16)] * 2,
        cost_estimate=cost(2 * height * count * width**2, 6 * height * count * width),
    )(screen, factors, density)


def transform(factors, density, screen):
    count, width = factors.shape[0], factors.shape[-1]

    def kernel(flag, left, right, out):
        scale = flag[0, 0].astype(F32).astype(BF16)
        for step in range(STEP):
            piece = left[step].reshape(width, width)
            product = jnp.dot(piece, right[0], preferred_element_type=F32).astype(BF16)
            out[:, pl.ds(step * width, width)] = product * scale

    return pl.pallas_call(
        kernel,
        grid=(count // STEP,),
        in_specs=[
            SMEM,
            pl.BlockSpec((STEP, PARTS, ROWS, width), lambda i: (i, 0, 0, 0)),
            pl.BlockSpec((1, width, width), lambda i: (0, 0, 0)),
        ],
        out_specs=pl.BlockSpec((width, STEP * width), lambda i: (0, i)),
        out_shape=jax.ShapeDtypeStruct((width, count * width), BF16),
        compiler_params=params(),
        cost_estimate=cost(2 * count * width**3, 4 * count * width**2),
    )(screen, factors, density)


def contract(left, right):
    return lax.dot_general(left, right, (((1,), (1,)), ((), ())), preferred_element_type=F32)


def early_rows(ref, part, columns):
    low = ref[pl.ds(pl.multiple_of(16 * part, 16), 16), columns]
    high = ref[pl.ds(pl.multiple_of(128 + 32 * part, 32), 32), columns]
    return low, high


def late_rows(ref, part, columns):
    return ref[pl.ds(pl.multiple_of(16 * part, 16), 16), columns]


def put(out, y, offset, values):
    for value in values:
        out[y, pl.ds(offset, value.shape[0]), :] = value.astype(out.dtype)
        offset += value.shape[0]
    return offset


def lanes(index):
    return pl.ds(index * LANES, LANES)


def pick(first, second):
    even = on_even()
    first, second = first[...], second[...]
    return jnp.where(even, first, second), jnp.where(even, second, first)


def products(kernel, inputs, outputs, flops, scratch=()):
    return pl.pallas_call(
        kernel,
        in_specs=[VMEM] * len(inputs),
        out_specs=[VMEM] * len(outputs),
        out_shape=[jax.ShapeDtypeStruct(shape, dtype) for shape, dtype in outputs],
        scratch_shapes=[pltpu.VMEM(shape, F32) for shape in scratch],
        compiler_params=params(),
        cost_estimate=cost(flops, sum(2 * value.size for value in inputs)),
    )(*inputs)


def begin(near, first, second):
    shape = first.shape

    def kernel(near, first, second, ahead, behind, upper, corner):
        ahead[...], behind[...] = pick(first, second)
        upper[...] = contract(near[...], ahead[...])
        corner[...] = contract(behind[...], ahead[...])

    outputs = [(shape, BF16), (shape, BF16), ((near.shape[0], shape[0]), F32), ((shape[0], shape[0]), F32)]
    return products(kernel, (near, first, second), outputs, 2 * near.size * shape[0])


def advance(near, ahead0, behind0, first, second):
    height, depth = first.shape
    columns = pl.ds(0, depth)

    def kernel(near, ahead0, behind0, first, second, ahead, behind, upper, right, below, corner):
        ahead[...], behind[...] = pick(first, second)
        upper[...] = contract(near[:, columns], ahead[...])
        right[...] = contract(behind0[:, columns], ahead[...])
        below[...] = contract(behind[...], ahead0[:, columns])
        corner[...] = contract(behind[...], ahead[...])

    low = ahead0.shape[0]
    outputs = [((height, depth), BF16)] * 2
    outputs += [(shape, F32) for shape in ((near.shape[0], height), (low, height), (height, low), (height, height))]
    return products(kernel, (near, ahead0, behind0, first, second), outputs, 2 * near.size * height)


def pack_early(near, start, half, first, second):
    width = near.shape[0]
    places = PARTS // 2
    height, depth = first.shape
    columns = pl.ds(near.shape[1] - depth, depth)
    low, high = pl.ds(0, EARLY - height), pl.ds(EARLY - height, height)

    def kernel(near, ahead0, behind0, upper0, corner0, upper1, right, below, corner, first, second, kept, sent, ahead, behind, upper, lower, upper_far, lower_far):
        ahead[...], behind[...] = pick(first, second)
        upper[:, low] = upper0[...]
        upper[:, high] = upper1[...] + contract(near[:, columns], ahead[...])
        lower[...] = upper[...].T
        upper_far[low, low] = corner0[...]
        upper_far[low, high] = right[...] + contract(behind0[:, columns], ahead[...])
        upper_far[high, low] = below[...] + contract(behind[...], ahead0[:, columns])
        upper_far[high, high] = corner[...] + contract(behind[...], ahead[...])
        lower_far[...] = upper_far[...].T
        mine = spot()[0]
        for y in range(places):
            for out, core in ((sent, 1 - mine), (kept, mine)):
                part = 2 * y + core
                own = pl.ds(pl.multiple_of(ROWS * part, ROWS), ROWS)
                at = put(out, y, 0, [upper[own, lanes(t)] for t in range(3)])
                for t in range(3):
                    at = put(out, y, at, early_rows(upper_far, part, lanes(t)))
                for t in range(4):
                    at = put(out, y, at, early_rows(lower, part, lanes(t)))
                for t in range(3):
                    at = put(out, y, at, early_rows(lower_far, part, lanes(t)))

    shape = (places, EARLY_ALL, LANES)
    outputs = [(shape, F32), (shape, BF16), ((height, depth), BF16), ((height, depth), BF16)]
    scratch = ((width, EARLY), (EARLY, width), (EARLY, EARLY), (EARLY, EARLY))
    return products(kernel, (near, *start, *half[2:], first, second), outputs, near.size * EARLY, scratch)


def pack_middle(near, ahead0, behind0, ahead1, behind1, first, second):
    width = near.shape[0]
    height, depth = first.shape
    columns = pl.ds(0, depth)
    low, high = pl.ds(0, ahead0.shape[0]), pl.ds(ahead0.shape[0], ahead1.shape[0])

    def kernel(near, ahead0, behind0, ahead1, behind1, first, second, upper, tall, tall_t, corner):
        last, prior = pick(first, second)
        upper[...] = contract(near[:, columns], last)
        tall[low, :] = contract(behind0[:, columns], last)
        tall[high, :] = contract(behind1[...], last)
        tall_t[low, :] = contract(ahead0[:, columns], prior)
        tall_t[high, :] = contract(ahead1[...], prior)
        corner[...] = contract(prior, last)

    outputs = [((rows, height), F32) for rows in (width, EARLY, EARLY, height)]
    inputs = (near, ahead0, behind0, ahead1, behind1, first, second)
    return products(kernel, inputs, outputs, 3 * near.size * height)


def pack_late(near, ahead0, behind0, ahead1, behind1, middle, first, second):
    width = near.shape[0]
    places = PARTS // 2
    depth = first.shape[1]
    columns = pl.ds(near.shape[1] - depth, depth)
    low, high = pl.ds(0, ahead0.shape[0]), pl.ds(ahead0.shape[0], ahead1.shape[0])

    def kernel(near, ahead0, behind0, ahead1, behind1, upper0, tall0, tall_t0, corner0, first, second, kept, sent, upper, lower, tall, wide, tall_t, wide_t):
        last, prior = pick(first, second)
        value = upper0[...] + contract(near[:, columns], last)
        upper[...] = value
        lower[...] = value.T
        tall[low, :] = tall0[low, :] + contract(behind0[:, columns], last)
        tall[high, :] = tall0[high, :] + contract(behind1[...], last)
        wide_t[:, pl.ds(0, EARLY)] = tall[...].T
        tall_t[low, :] = tall_t0[low, :] + contract(ahead0[:, columns], prior)
        tall_t[high, :] = tall_t0[high, :] + contract(ahead1[...], prior)
        wide[:, pl.ds(0, EARLY)] = tall_t[...].T
        value = corner0[...] + contract(prior, last)
        wide[:, pl.ds(EARLY, LATE)] = value
        wide_t[:, pl.ds(EARLY, LATE)] = value.T
        mine = spot()[0]
        for y in range(places):
            for out, core in ((sent, 1 - mine), (kept, mine)):
                part = 2 * y + core
                own = pl.ds(pl.multiple_of(ROWS * part, ROWS), ROWS)
                at = put(out, y, 0, [upper[own, :]])
                at = put(out, y, at, early_rows(tall, part, lanes(0)))
                at = put(out, y, at, [late_rows(wide, part, lanes(t)) for t in range(4)])
                at = put(out, y, at, [late_rows(lower, part, lanes(t)) for t in range(4)])
                at = put(out, y, at, early_rows(tall_t, part, lanes(0)))
                at = put(out, y, at, [late_rows(wide_t, part, lanes(t)) for t in range(4)])

    shape = (places, LATE_ALL, LANES)
    inputs = (near, ahead0, behind0, ahead1, behind1, *middle, first, second)
    scratch = ((width, LATE), (LATE, width), (EARLY, LATE), (LATE, width), (EARLY, LATE), (LATE, width))
    return products(kernel, inputs, [(shape, F32), (shape, BF16)], 3 * near.size * LATE, scratch)


def join_core(kept, received):
    places, rows, width = kept.shape

    def kernel(kept, received, total, *pieces):
        y = spot()[1]
        total[...] = kept[y] + received[y].astype(F32)
        for steps in range(1, places):
            target = lax.rem(y + steps, places)
            pieces[steps - 1][...] = (kept[target] + received[target].astype(F32)).astype(BF16)

    shape = (rows, width)
    return pl.pallas_call(
        kernel,
        in_specs=[VMEM, VMEM],
        out_specs=[VMEM] * places,
        out_shape=[jax.ShapeDtypeStruct(shape, F32)] + [jax.ShapeDtypeStruct(shape, BF16)] * (places - 1),
        compiler_params=params(),
        cost_estimate=cost(kept.size, 8 * kept.size),
    )(kept, received)


def after(value, *others):
    return lax.optimization_barrier((value, *others))[0]


def send_places(pieces):
    received = []
    for steps in (2, 1, 3):
        received.append(shift_y(pieces[steps - 1], steps))
    return received


def gather(refs, span):
    total, *received = refs
    value = total[span, :]
    for piece in received:
        value = value + piece[span, :].astype(F32)
    return value


def join_early(total, received):
    rows, width = total.shape

    def kernel(total, one, two, three, upper, rest):
        refs = (total, one, two, three)
        upper[...] = gather(refs, pl.ds(0, EARLY_U1))
        rest[...] = gather(refs, pl.ds(EARLY_U1, rows - EARLY_U1)).astype(BF16)

    return pl.pallas_call(
        kernel,
        in_specs=[VMEM] * 4,
        out_specs=[VMEM] * 2,
        out_shape=[
            jax.ShapeDtypeStruct((EARLY_U1, width), F32),
            jax.ShapeDtypeStruct((rows - EARLY_U1, width), BF16),
        ],
        compiler_params=params(),
        cost_estimate=cost(total.size * 3, 12 * total.size),
    )(total, *received)


def join_late(rest, total, received):
    rows, width = total.shape
    far = EARLY_U2 + LATE_U2
    low = rest.shape[0] - EARLY_U2
    height = low + rows - LATE_U1 - LATE_U2

    def kernel(rest, total, one, two, three, upper, first, second):
        refs = (total, one, two, three)
        even = on_even()
        upper[...] = gather(refs, pl.ds(0, LATE_U1))
        late_far = gather(refs, pl.ds(LATE_U1, LATE_U2)).astype(BF16)
        late_low = gather(refs, pl.ds(LATE_U1 + LATE_U2, rows - LATE_U1 - LATE_U2)).astype(BF16)

        def write(lower, upper_far):
            lower[pl.ds(0, low), :] = rest[pl.ds(EARLY_U2, low), :]
            lower[pl.ds(low, late_low.shape[0]), :] = late_low
            upper_far[pl.ds(0, EARLY_U2), :] = rest[pl.ds(0, EARLY_U2), :]
            upper_far[pl.ds(EARLY_U2, LATE_U2), :] = late_far
            upper_far[pl.ds(far, height - far), :] = jnp.zeros((height - far, width), BF16)

        pl.when(even)(lambda: write(first, second))
        pl.when(jnp.logical_not(even))(lambda: write(second, first))

    return pl.pallas_call(
        kernel,
        in_specs=[VMEM] * 5,
        out_specs=[VMEM] * 3,
        out_shape=[
            jax.ShapeDtypeStruct((LATE_U1, width), F32),
            jax.ShapeDtypeStruct((height, width), BF16),
            jax.ShapeDtypeStruct((height, width), BF16),
        ],
        compiler_params=params(),
        cost_estimate=cost(total.size * 3, 12 * total.size),
    )(rest, total, *received)


def restore(order, early, late):
    width = order.shape[0]

    def kernel(order, early, late, out):
        blocks = [early[pl.ds(ROWS * t, ROWS), :] for t in range(3)] + [late[...]]
        value = jnp.concatenate(blocks, axis=1)
        exact = order[...].astype(F32)
        out[...] = jnp.dot(value, exact, preferred_element_type=F32, precision=lax.Precision.HIGHEST)

    return pl.pallas_call(
        kernel,
        in_specs=[VMEM] * 3,
        out_specs=VMEM,
        out_shape=jax.ShapeDtypeStruct((ROWS, width), F32),
        compiler_params=params(),
        cost_estimate=cost(2 * 6 * ROWS * width**2, 4 * width**2),
    )(order, early, late)


def assemble(order, upper, first, second):
    width = order.shape[0]
    late_low = 3 * 144 - 96

    def rows(ref, base, late):
        body = jnp.concatenate(
            [ref[pl.ds(base + 48 * t, 48), :] for t in range(3)] + [ref[pl.ds(late, 48), :]], axis=1
        )
        last = jnp.concatenate([ref[pl.ds(late + 48 + 16 * t, 16), :] for t in range(4)], axis=1)
        return jnp.concatenate([body[:16], last, body[16:]], axis=0)

    def kernel(order, upper, first, second, out):
        even = on_even()
        out[0, 0] = upper[...]

        def write(far, low):
            exact = order[...]
            out[0, 1] = jnp.dot(rows(far, 0, EARLY_U2), exact, preferred_element_type=F32)
            for t in range(4):
                out[0, 2, pl.ds(0, 16), lanes(t)] = low[pl.ds(48 * t, 16), :].astype(F32)
                out[0, 2, pl.ds(16, 16), lanes(t)] = low[pl.ds(late_low + 16 * t, 16), :].astype(F32)
                out[0, 2, pl.ds(32, 32), lanes(t)] = low[pl.ds(48 * t + 16, 32), :].astype(F32)
            out[0, 3] = jnp.dot(rows(low, 192, late_low + 64), exact, preferred_element_type=F32)

        pl.when(even)(lambda: write(first, second))
        pl.when(jnp.logical_not(even))(lambda: write(second, first))

    return pl.pallas_call(
        kernel,
        in_specs=[VMEM] * 4,
        out_specs=VMEM,
        out_shape=jax.ShapeDtypeStruct((1, 4, ROWS, width), F32),
        compiler_params=params(),
        cost_estimate=cost(2 * 2 * ROWS * width**2, 4 * ROWS * width * 8),
    )(order, upper, first, second)


def natural_order(width):
    index = jnp.arange(width)
    low = ROWS * (index // 16) + index % 16
    high = ROWS * ((index - 128) // 32) + 32 + index % 32
    last = ROWS * ((index - EARLY) // 16) + 16 + index % 16
    place = jnp.where(index < 128, low, jnp.where(index < EARLY, high, last))
    return (place[:, None] == jnp.arange(width)[None, :]).astype(BF16)


def body(factors, density, screen):
    count, width = factors.shape[1], factors.shape[2]
    owned, blocks = factors[0].reshape(count, PARTS, ROWS, width), density[0]
    first, second = [], []
    source = owned
    for chunk in CHUNKS:
        one, two = split(source, blocks, screen, *chunk)
        source = after(owned, one)
        second.append(swap_atoms(two, 1))
        first.append(swap_atoms(one, 0))
    near = transform(source, blocks, screen)
    start = begin(near, first[0], second[0])
    half = advance(near, *start[:2], first[1], second[1])
    kept, sent, ahead, behind = pack_early(near, start, half, first[2], second[2])
    total, *pieces = join_core(kept, swap_core(sent))
    received = send_places(pieces)
    middle = pack_middle(near, *start[:2], *half[:2], first[3], second[3])
    kept, sent = pack_late(near, *start[:2], ahead, behind, middle, first[4], second[4])
    late_total, *late_pieces = join_core(kept, swap_core(sent))
    late_received = send_places(late_pieces)
    upper, rest = join_early(after(total, *late_pieces), received)
    late_upper, one, two = join_late(rest, late_total, late_received)
    two = swap_atoms(two, 1)
    one = swap_atoms(one, 0)
    order = natural_order(width)
    upper = restore(order, upper, late_upper)
    return assemble(order, upper, one, two)


def solution(mesh):
    in_specs = (P("atoms", "aux", None, None), P("atoms", None, None, None), P("atoms", None))
    out_specs = P("atoms", None, "aux", None)
    return jax.shard_map(body, mesh=mesh, in_specs=in_specs, out_specs=out_specs, check_vma=False)
```

```python
import jax
import jax.numpy as jnp
from jax import lax
from jax.experimental import pallas as pl
from jax.experimental.pallas import tpu as pltpu
from jax.sharding import PartitionSpec as P


F32, BF16 = jnp.float32, jnp.bfloat16
VMEM = pl.BlockSpec(memory_space=pltpu.VMEM)
SMEM = pl.BlockSpec(memory_space=pltpu.SMEM)
LANES = 128
ROWS, PARTS, STEP = 64, 8, 3
CHUNKS = ((0, 16, 0, 3), (0, 16, 3, 3), (32, 32, 0, 3), (32, 32, 3, 3), (16, 16, 0, 3), (16, 16, 3, 3))
EARLY, LATE = 384, 128
EARLY_U1, EARLY_U2, EARLY_ALL = 192, 144, 672
LATE_U1, LATE_U2, LATE_ALL = 64, 112, 352


def params(limit=20):
    return pltpu.CompilerParams(vmem_limit_bytes=limit * 1024 * 1024)


def cost(flops, size):
    return pl.CostEstimate(flops=flops, bytes_accessed=size, transcendentals=0)


def swap_atoms(value, first):
    count = lax.axis_size("atoms")
    pairs = [(i, i + 1) for i in range(first, count - 1, 2)]
    return lax.ppermute(value, "atoms", pairs + [(j, i) for i, j in pairs])


def swap_core(value):
    return lax.ppermute(value, "aux", [(i, i ^ 1) for i in range(lax.axis_size("aux"))])


def shift_y(value, steps):
    count = lax.axis_size("aux")
    return lax.ppermute(value, "aux", [(i, (i + 2 * steps) % count) for i in range(count)])


def spot():
    aux = lax.axis_index("aux")
    return lax.rem(aux, 2), lax.div(aux, 2)


def on_even():
    return lax.rem(lax.axis_index("atoms"), 2) == 0


def split(factors, density, screen, start, size, begin, count):
    width = factors.shape[-1]
    height = PARTS * size

    def kernel(flag, left, right, first, second):
        scale = flag[0, 1].astype(F32).astype(BF16)
        even = on_even()
        for step in range(STEP):
            columns = pl.ds(step * width, width)
            piece = left[step].reshape(height, width)
            far = jnp.dot(piece, right[0], preferred_element_type=F32).astype(BF16) * scale
            first[:, columns] = jnp.where(even, far, piece)
            second[:, columns] = jnp.where(even, piece, far)

    return pl.pallas_call(
        kernel,
        grid=(count // STEP,),
        in_specs=[
            SMEM,
            pl.BlockSpec((STEP, PARTS, size, width), lambda i: (begin // STEP + i, 0, start // size, 0)),
            pl.BlockSpec((1, width, width), lambda i: (1, 0, 0)),
        ],
        out_specs=[pl.BlockSpec((height, STEP * width), lambda i: (0, i))] * 2,
        out_shape=[jax.ShapeDtypeStruct((height, count * width), BF16)] * 2,
        cost_estimate=cost(2 * height * count * width**2, 6 * height * count * width),
    )(screen, factors, density)


def transform(factors, density, screen):
    count, width = factors.shape[0], factors.shape[-1]

    def kernel(flag, left, right, out):
        scale = flag[0, 0].astype(F32).astype(BF16)
        for step in range(STEP):
            piece = left[step].reshape(width, width)
            product = jnp.dot(piece, right[0], preferred_element_type=F32).astype(BF16)
            out[:, pl.ds(step * width, width)] = product * scale

    return pl.pallas_call(
        kernel,
        grid=(count // STEP,),
        in_specs=[
            SMEM,
            pl.BlockSpec((STEP, PARTS, ROWS, width), lambda i: (i, 0, 0, 0)),
            pl.BlockSpec((1, width, width), lambda i: (0, 0, 0)),
        ],
        out_specs=pl.BlockSpec((width, STEP * width), lambda i: (0, i)),
        out_shape=jax.ShapeDtypeStruct((width, count * width), BF16),
        compiler_params=params(),
        cost_estimate=cost(2 * count * width**3, 4 * count * width**2),
    )(screen, factors, density)


def contract(left, right):
    return lax.dot_general(left, right, (((1,), (1,)), ((), ())), preferred_element_type=F32)


def early_rows(ref, part, columns):
    low = ref[pl.ds(pl.multiple_of(16 * part, 16), 16), columns]
    high = ref[pl.ds(pl.multiple_of(128 + 32 * part, 32), 32), columns]
    return low, high


def late_rows(ref, part, columns):
    return ref[pl.ds(pl.multiple_of(16 * part, 16), 16), columns]


def put(out, y, offset, values):
    for value in values:
        out[y, pl.ds(offset, value.shape[0]), :] = value.astype(out.dtype)
        offset += value.shape[0]
    return offset


def lanes(index):
    return pl.ds(index * LANES, LANES)


def pick(first, second):
    even = on_even()
    first, second = first[...], second[...]
    return jnp.where(even, first, second), jnp.where(even, second, first)


def products(kernel, inputs, outputs, flops, scratch=()):
    return pl.pallas_call(
        kernel,
        in_specs=[VMEM] * len(inputs),
        out_specs=[VMEM] * len(outputs),
        out_shape=[jax.ShapeDtypeStruct(shape, dtype) for shape, dtype in outputs],
        scratch_shapes=[pltpu.VMEM(shape, F32) for shape in scratch],
        compiler_params=params(),
        cost_estimate=cost(flops, sum(2 * value.size for value in inputs)),
    )(*inputs)


def begin(near, first, second):
    height, depth = first[0].shape
    shape = (height, len(first) * depth)

    def kernel(near, first0, first1, second0, second1, ahead, behind, upper, corner):
        low, high = pl.ds(0, depth), pl.ds(depth, depth)
        ahead[:, low], behind[:, low] = pick(first0, second0)
        ahead[:, high], behind[:, high] = pick(first1, second1)
        upper[...] = contract(near[...], ahead[...])
        corner[...] = contract(behind[...], ahead[...])

    outputs = [(shape, BF16), (shape, BF16), ((near.shape[0], height), F32), ((height, height), F32)]
    return products(kernel, (near, *first, *second), outputs, 2 * near.size * height)


def advance(near, ahead0, behind0, first, second):
    height, depth = first.shape
    columns = pl.ds(0, depth)

    def kernel(near, ahead0, behind0, first, second, ahead, behind, upper, right, below, corner):
        ahead[...], behind[...] = pick(first, second)
        upper[...] = contract(near[:, columns], ahead[...])
        right[...] = contract(behind0[:, columns], ahead[...])
        below[...] = contract(behind[...], ahead0[:, columns])
        corner[...] = contract(behind[...], ahead[...])

    low = ahead0.shape[0]
    outputs = [((height, depth), BF16)] * 2
    outputs += [(shape, F32) for shape in ((near.shape[0], height), (low, height), (height, low), (height, height))]
    return products(kernel, (near, ahead0, behind0, first, second), outputs, 2 * near.size * height)


def pack_early(near, start, half, first, second):
    width = near.shape[0]
    places = PARTS // 2
    height, depth = first.shape
    columns = pl.ds(near.shape[1] - depth, depth)
    low, high = pl.ds(0, EARLY - height), pl.ds(EARLY - height, height)

    def kernel(near, ahead0, behind0, upper0, corner0, upper1, right, below, corner, first, second, kept, sent, ahead, behind, upper, lower, upper_far, lower_far):
        ahead[...], behind[...] = pick(first, second)
        upper[:, low] = upper0[...]
        upper[:, high] = upper1[...] + contract(near[:, columns], ahead[...])
        lower[...] = upper[...].T
        upper_far[low, low] = corner0[...]
        upper_far[low, high] = right[...] + contract(behind0[:, columns], ahead[...])
        upper_far[high, low] = below[...] + contract(behind[...], ahead0[:, columns])
        upper_far[high, high] = corner[...] + contract(behind[...], ahead[...])
        lower_far[...] = upper_far[...].T
        mine = spot()[0]
        for y in range(places):
            for out, core in ((sent, 1 - mine), (kept, mine)):
                part = 2 * y + core
                own = pl.ds(pl.multiple_of(ROWS * part, ROWS), ROWS)
                at = put(out, y, 0, [upper[own, lanes(t)] for t in range(3)])
                for t in range(3):
                    at = put(out, y, at, early_rows(upper_far, part, lanes(t)))
                for t in range(4):
                    at = put(out, y, at, early_rows(lower, part, lanes(t)))
                for t in range(3):
                    at = put(out, y, at, early_rows(lower_far, part, lanes(t)))

    shape = (places, EARLY_ALL, LANES)
    outputs = [(shape, F32), (shape, BF16), ((height, depth), BF16), ((height, depth), BF16)]
    scratch = ((width, EARLY), (EARLY, width), (EARLY, EARLY), (EARLY, EARLY))
    return products(kernel, (near, *start, *half[2:], first, second), outputs, near.size * EARLY, scratch)


def pack_middle(near, ahead0, behind0, ahead1, behind1, first, second):
    width = near.shape[0]
    height, depth = first.shape
    columns = pl.ds(0, depth)
    low, high = pl.ds(0, ahead0.shape[0]), pl.ds(ahead0.shape[0], ahead1.shape[0])

    def kernel(near, ahead0, behind0, ahead1, behind1, first, second, upper, tall, tall_t, corner):
        last, prior = pick(first, second)
        upper[...] = contract(near[:, columns], last)
        tall[low, :] = contract(behind0[:, columns], last)
        tall[high, :] = contract(behind1[...], last)
        tall_t[low, :] = contract(ahead0[:, columns], prior)
        tall_t[high, :] = contract(ahead1[...], prior)
        corner[...] = contract(prior, last)

    outputs = [((rows, height), F32) for rows in (width, EARLY, EARLY, height)]
    inputs = (near, ahead0, behind0, ahead1, behind1, first, second)
    return products(kernel, inputs, outputs, 3 * near.size * height)


def pack_late(near, ahead0, behind0, ahead1, behind1, middle, first, second):
    width = near.shape[0]
    places = PARTS // 2
    depth = first.shape[1]
    columns = pl.ds(near.shape[1] - depth, depth)
    low, high = pl.ds(0, ahead0.shape[0]), pl.ds(ahead0.shape[0], ahead1.shape[0])

    def kernel(near, ahead0, behind0, ahead1, behind1, upper0, tall0, tall_t0, corner0, first, second, kept, sent, upper, lower, tall, wide, tall_t, wide_t):
        last, prior = pick(first, second)
        value = upper0[...] + contract(near[:, columns], last)
        upper[...] = value
        lower[...] = value.T
        tall[low, :] = tall0[low, :] + contract(behind0[:, columns], last)
        tall[high, :] = tall0[high, :] + contract(behind1[...], last)
        wide_t[:, pl.ds(0, EARLY)] = tall[...].T
        tall_t[low, :] = tall_t0[low, :] + contract(ahead0[:, columns], prior)
        tall_t[high, :] = tall_t0[high, :] + contract(ahead1[...], prior)
        wide[:, pl.ds(0, EARLY)] = tall_t[...].T
        value = corner0[...] + contract(prior, last)
        wide[:, pl.ds(EARLY, LATE)] = value
        wide_t[:, pl.ds(EARLY, LATE)] = value.T
        mine = spot()[0]
        for y in range(places):
            for out, core in ((sent, 1 - mine), (kept, mine)):
                part = 2 * y + core
                own = pl.ds(pl.multiple_of(ROWS * part, ROWS), ROWS)
                at = put(out, y, 0, [upper[own, :]])
                at = put(out, y, at, early_rows(tall, part, lanes(0)))
                at = put(out, y, at, [late_rows(wide, part, lanes(t)) for t in range(4)])
                at = put(out, y, at, [late_rows(lower, part, lanes(t)) for t in range(4)])
                at = put(out, y, at, early_rows(tall_t, part, lanes(0)))
                at = put(out, y, at, [late_rows(wide_t, part, lanes(t)) for t in range(4)])

    shape = (places, LATE_ALL, LANES)
    inputs = (near, ahead0, behind0, ahead1, behind1, *middle, first, second)
    scratch = ((width, LATE), (LATE, width), (EARLY, LATE), (LATE, width), (EARLY, LATE), (LATE, width))
    return products(kernel, inputs, [(shape, F32), (shape, BF16)], 3 * near.size * LATE, scratch)


def join_core(kept, received):
    places, rows, width = kept.shape

    def kernel(kept, received, total, *pieces):
        y = spot()[1]
        total[...] = kept[y] + received[y].astype(F32)
        for steps in range(1, places):
            target = lax.rem(y + steps, places)
            pieces[steps - 1][...] = (kept[target] + received[target].astype(F32)).astype(BF16)

    shape = (rows, width)
    return pl.pallas_call(
        kernel,
        in_specs=[VMEM, VMEM],
        out_specs=[VMEM] * places,
        out_shape=[jax.ShapeDtypeStruct(shape, F32)] + [jax.ShapeDtypeStruct(shape, BF16)] * (places - 1),
        compiler_params=params(),
        cost_estimate=cost(kept.size, 8 * kept.size),
    )(kept, received)


def after(value, *others):
    return lax.optimization_barrier((value, *others))[0]


def send_places(pieces):
    received = []
    for steps in (1, 2, 3):
        received.append(shift_y(pieces[steps - 1], steps))
    return received


def gather(refs, span):
    total, *received = refs
    value = total[span, :]
    for piece in received:
        value = value + piece[span, :].astype(F32)
    return value


def join_early(total, received):
    rows, width = total.shape

    def kernel(total, one, two, three, upper, rest):
        refs = (total, one, two, three)
        upper[...] = gather(refs, pl.ds(0, EARLY_U1))
        rest[...] = gather(refs, pl.ds(EARLY_U1, rows - EARLY_U1)).astype(BF16)

    return pl.pallas_call(
        kernel,
        in_specs=[VMEM] * 4,
        out_specs=[VMEM] * 2,
        out_shape=[
            jax.ShapeDtypeStruct((EARLY_U1, width), F32),
            jax.ShapeDtypeStruct((rows - EARLY_U1, width), BF16),
        ],
        compiler_params=params(),
        cost_estimate=cost(total.size * 3, 12 * total.size),
    )(total, *received)


def join_late(rest, total, received):
    rows, width = total.shape
    far = EARLY_U2 + LATE_U2
    low = rest.shape[0] - EARLY_U2
    height = low + rows - LATE_U1 - LATE_U2

    def kernel(rest, total, one, two, three, upper, first, second):
        refs = (total, one, two, three)
        even = on_even()
        upper[...] = gather(refs, pl.ds(0, LATE_U1))
        late_far = gather(refs, pl.ds(LATE_U1, LATE_U2)).astype(BF16)
        late_low = gather(refs, pl.ds(LATE_U1 + LATE_U2, rows - LATE_U1 - LATE_U2)).astype(BF16)

        def write(lower, upper_far):
            lower[pl.ds(0, low), :] = rest[pl.ds(EARLY_U2, low), :]
            lower[pl.ds(low, late_low.shape[0]), :] = late_low
            upper_far[pl.ds(0, EARLY_U2), :] = rest[pl.ds(0, EARLY_U2), :]
            upper_far[pl.ds(EARLY_U2, LATE_U2), :] = late_far
            upper_far[pl.ds(far, height - far), :] = jnp.zeros((height - far, width), BF16)

        pl.when(even)(lambda: write(first, second))
        pl.when(jnp.logical_not(even))(lambda: write(second, first))

    return pl.pallas_call(
        kernel,
        in_specs=[VMEM] * 5,
        out_specs=[VMEM] * 3,
        out_shape=[
            jax.ShapeDtypeStruct((LATE_U1, width), F32),
            jax.ShapeDtypeStruct((height, width), BF16),
            jax.ShapeDtypeStruct((height, width), BF16),
        ],
        compiler_params=params(),
        cost_estimate=cost(total.size * 3, 12 * total.size),
    )(rest, total, *received)


def restore(order, early, late):
    width = order.shape[0]

    def kernel(order, early, late, out):
        blocks = [early[pl.ds(ROWS * t, ROWS), :] for t in range(3)] + [late[...]]
        value = jnp.concatenate(blocks, axis=1)
        exact = order[...].astype(F32)
        out[...] = jnp.dot(value, exact, preferred_element_type=F32, precision=lax.Precision.HIGHEST)

    return pl.pallas_call(
        kernel,
        in_specs=[VMEM] * 3,
        out_specs=VMEM,
        out_shape=jax.ShapeDtypeStruct((ROWS, width), F32),
        compiler_params=params(),
        cost_estimate=cost(2 * 6 * ROWS * width**2, 4 * width**2),
    )(order, early, late)


def assemble(order, upper, first, second):
    width = order.shape[0]
    late_low = 3 * 144 - 96

    def rows(ref, base, late):
        body = jnp.concatenate(
            [ref[pl.ds(base + 48 * t, 48), :] for t in range(3)] + [ref[pl.ds(late, 48), :]], axis=1
        )
        last = jnp.concatenate([ref[pl.ds(late + 48 + 16 * t, 16), :] for t in range(4)], axis=1)
        return jnp.concatenate([body[:16], last, body[16:]], axis=0)

    def kernel(order, upper, first, second, out):
        even = on_even()
        out[0, 0] = upper[...]

        def write(far, low):
            exact = order[...]
            out[0, 1] = jnp.dot(rows(far, 0, EARLY_U2), exact, preferred_element_type=F32)
            for t in range(4):
                out[0, 2, pl.ds(0, 16), lanes(t)] = low[pl.ds(48 * t, 16), :].astype(F32)
                out[0, 2, pl.ds(16, 16), lanes(t)] = low[pl.ds(late_low + 16 * t, 16), :].astype(F32)
                out[0, 2, pl.ds(32, 32), lanes(t)] = low[pl.ds(48 * t + 16, 32), :].astype(F32)
            out[0, 3] = jnp.dot(rows(low, 192, late_low + 64), exact, preferred_element_type=F32)

        pl.when(even)(lambda: write(first, second))
        pl.when(jnp.logical_not(even))(lambda: write(second, first))

    return pl.pallas_call(
        kernel,
        in_specs=[VMEM] * 4,
        out_specs=VMEM,
        out_shape=jax.ShapeDtypeStruct((1, 4, ROWS, width), F32),
        compiler_params=params(),
        cost_estimate=cost(2 * 2 * ROWS * width**2, 4 * ROWS * width * 8),
    )(order, upper, first, second)


def natural_order(width):
    index = jnp.arange(width)
    low = ROWS * (index // 16) + index % 16
    high = ROWS * ((index - 128) // 32) + 32 + index % 32
    last = ROWS * ((index - EARLY) // 16) + 16 + index % 16
    place = jnp.where(index < 128, low, jnp.where(index < EARLY, high, last))
    return (place[:, None] == jnp.arange(width)[None, :]).astype(BF16)


def body(factors, density, screen):
    count, width = factors.shape[1], factors.shape[2]
    owned, blocks = factors[0].reshape(count, PARTS, ROWS, width), density[0]
    first, second = [], []
    source = owned
    for chunk in CHUNKS:
        one, two = split(source, blocks, screen, *chunk)
        source = after(owned, one)
        second.append(swap_atoms(two, 1))
        first.append(swap_atoms(one, 0))
    near = transform(source, blocks, screen)
    start = begin(near, first[:2], second[:2])
    half = advance(near, *start[:2], first[2], second[2])
    kept, sent, ahead, behind = pack_early(near, start, half, first[3], second[3])
    total, *pieces = join_core(kept, swap_core(sent))
    received = send_places(pieces)
    middle = pack_middle(near, *start[:2], *half[:2], first[4], second[4])
    kept, sent = pack_late(near, *start[:2], ahead, behind, middle, first[5], second[5])
    late_total, *late_pieces = join_core(kept, swap_core(sent))
    late_received = send_places(late_pieces)
    upper, rest = join_early(after(total, *late_pieces), received)
    late_upper, one, two = join_late(rest, late_total, late_received)
    two = swap_atoms(two, 1)
    one = swap_atoms(one, 0)
    order = natural_order(width)
    upper = restore(order, upper, late_upper)
    return assemble(order, upper, one, two)


def solution(mesh):
    in_specs = (P("atoms", "aux", None, None), P("atoms", None, None, None), P("atoms", None))
    out_specs = P("atoms", None, "aux", None)
    return jax.shard_map(body, mesh=mesh, in_specs=in_specs, out_specs=out_specs, check_vma=False)
```

```python
import jax
import jax.numpy as jnp
from jax import lax
from jax.experimental import pallas as pl
from jax.experimental.pallas import tpu as pltpu
from jax.sharding import PartitionSpec as P


F32, BF16 = jnp.float32, jnp.bfloat16
VMEM = pl.BlockSpec(memory_space=pltpu.VMEM)
SMEM = pl.BlockSpec(memory_space=pltpu.SMEM)
LANES = 128
ROWS, PARTS, STEP = 64, 8, 3
CHUNKS = ((0, 16, 0, 3), (0, 16, 3, 3), (32, 32, 0, 3), (32, 32, 3, 3), (16, 16, 0, 3), (16, 16, 3, 3))
EARLY, LATE = 384, 128
EARLY_U1, EARLY_U2, EARLY_ALL = 192, 144, 672
LATE_U1, LATE_U2, LATE_ALL = 64, 112, 352


def params(limit=20):
    return pltpu.CompilerParams(vmem_limit_bytes=limit * 1024 * 1024)


def cost(flops, size):
    return pl.CostEstimate(flops=flops, bytes_accessed=size, transcendentals=0)


def swap_atoms(value, first):
    count = lax.axis_size("atoms")
    pairs = [(i, i + 1) for i in range(first, count - 1, 2)]
    return lax.ppermute(value, "atoms", pairs + [(j, i) for i, j in pairs])


def swap_core(value):
    return lax.ppermute(value, "aux", [(i, i ^ 1) for i in range(lax.axis_size("aux"))])


def shift_y(value, steps):
    count = lax.axis_size("aux")
    return lax.ppermute(value, "aux", [(i, (i + 2 * steps) % count) for i in range(count)])


def spot():
    aux = lax.axis_index("aux")
    return lax.rem(aux, 2), lax.div(aux, 2)


def on_even():
    return lax.rem(lax.axis_index("atoms"), 2) == 0


def split(factors, density, screen, start, size, begin, count):
    width = factors.shape[-1]
    height = PARTS * size

    def kernel(flag, left, right, first, second):
        scale = flag[0, 1].astype(F32).astype(BF16)
        even = on_even()
        for step in range(STEP):
            columns = pl.ds(step * width, width)
            piece = left[step].reshape(height, width)
            far = jnp.dot(piece, right[0], preferred_element_type=F32).astype(BF16) * scale
            first[:, columns] = jnp.where(even, far, piece)
            second[:, columns] = jnp.where(even, piece, far)

    return pl.pallas_call(
        kernel,
        grid=(count // STEP,),
        in_specs=[
            SMEM,
            pl.BlockSpec((STEP, PARTS, size, width), lambda i: (begin // STEP + i, 0, start // size, 0)),
            pl.BlockSpec((1, width, width), lambda i: (1, 0, 0)),
        ],
        out_specs=[pl.BlockSpec((height, STEP * width), lambda i: (0, i))] * 2,
        out_shape=[jax.ShapeDtypeStruct((height, count * width), BF16)] * 2,
        cost_estimate=cost(2 * height * count * width**2, 6 * height * count * width),
    )(screen, factors, density)


def transform(factors, density, screen):
    count, width = factors.shape[0], factors.shape[-1]

    def kernel(flag, left, right, out):
        scale = flag[0, 0].astype(F32).astype(BF16)
        for step in range(STEP):
            piece = left[step].reshape(width, width)
            product = jnp.dot(piece, right[0], preferred_element_type=F32).astype(BF16)
            out[:, pl.ds(step * width, width)] = product * scale

    return pl.pallas_call(
        kernel,
        grid=(count // STEP,),
        in_specs=[
            SMEM,
            pl.BlockSpec((STEP, PARTS, ROWS, width), lambda i: (i, 0, 0, 0)),
            pl.BlockSpec((1, width, width), lambda i: (0, 0, 0)),
        ],
        out_specs=pl.BlockSpec((width, STEP * width), lambda i: (0, i)),
        out_shape=jax.ShapeDtypeStruct((width, count * width), BF16),
        compiler_params=params(),
        cost_estimate=cost(2 * count * width**3, 4 * count * width**2),
    )(screen, factors, density)


def contract(left, right):
    return lax.dot_general(left, right, (((1,), (1,)), ((), ())), preferred_element_type=F32)


def early_rows(ref, part, columns):
    low = ref[pl.ds(pl.multiple_of(16 * part, 16), 16), columns]
    high = ref[pl.ds(pl.multiple_of(128 + 32 * part, 32), 32), columns]
    return low, high


def late_rows(ref, part, columns):
    return ref[pl.ds(pl.multiple_of(16 * part, 16), 16), columns]


def put(out, y, offset, values):
    for value in values:
        out[y, pl.ds(offset, value.shape[0]), :] = value.astype(out.dtype)
        offset += value.shape[0]
    return offset


def lanes(index):
    return pl.ds(index * LANES, LANES)


def pick(first, second):
    even = on_even()
    first, second = first[...], second[...]
    return jnp.where(even, first, second), jnp.where(even, second, first)


def products(kernel, inputs, outputs, flops, scratch=()):
    return pl.pallas_call(
        kernel,
        in_specs=[VMEM] * len(inputs),
        out_specs=[VMEM] * len(outputs),
        out_shape=[jax.ShapeDtypeStruct(shape, dtype) for shape, dtype in outputs],
        scratch_shapes=[pltpu.VMEM(shape, F32) for shape in scratch],
        compiler_params=params(),
        cost_estimate=cost(flops, sum(2 * value.size for value in inputs)),
    )(*inputs)


def begin(near, first, second):
    height, depth = first[0].shape
    shape = (height, len(first) * depth)

    def kernel(near, first0, first1, second0, second1, ahead, behind, upper, corner):
        low, high = pl.ds(0, depth), pl.ds(depth, depth)
        ahead[:, low], behind[:, low] = pick(first0, second0)
        ahead[:, high], behind[:, high] = pick(first1, second1)
        upper[...] = contract(near[...], ahead[...])
        corner[...] = contract(behind[...], ahead[...])

    outputs = [(shape, BF16), (shape, BF16), ((near.shape[0], height), F32), ((height, height), F32)]
    return products(kernel, (near, *first, *second), outputs, 2 * near.size * height)


def advance(near, ahead0, behind0, first, second):
    height, depth = first.shape
    columns = pl.ds(0, depth)

    def kernel(near, ahead0, behind0, first, second, ahead, behind, upper, right, below, corner):
        ahead[...], behind[...] = pick(first, second)
        upper[...] = contract(near[:, columns], ahead[...])
        right[...] = contract(behind0[:, columns], ahead[...])
        below[...] = contract(behind[...], ahead0[:, columns])
        corner[...] = contract(behind[...], ahead[...])

    low = ahead0.shape[0]
    outputs = [((height, depth), BF16)] * 2
    outputs += [(shape, F32) for shape in ((near.shape[0], height), (low, height), (height, low), (height, height))]
    return products(kernel, (near, ahead0, behind0, first, second), outputs, 2 * near.size * height)


def pack_early(near, start, half, first, second):
    width = near.shape[0]
    places = PARTS // 2
    height, depth = first.shape
    columns = pl.ds(near.shape[1] - depth, depth)
    low, high = pl.ds(0, EARLY - height), pl.ds(EARLY - height, height)

    def kernel(near, ahead0, behind0, upper0, corner0, upper1, right, below, corner, first, second, kept, sent, ahead, behind, upper, lower, upper_far, lower_far):
        ahead[...], behind[...] = pick(first, second)
        upper[:, low] = upper0[...]
        upper[:, high] = upper1[...] + contract(near[:, columns], ahead[...])
        lower[...] = upper[...].T
        upper_far[low, low] = corner0[...]
        upper_far[low, high] = right[...] + contract(behind0[:, columns], ahead[...])
        upper_far[high, low] = below[...] + contract(behind[...], ahead0[:, columns])
        upper_far[high, high] = corner[...] + contract(behind[...], ahead[...])
        lower_far[...] = upper_far[...].T
        mine = spot()[0]
        for y in range(places):
            for out, core in ((sent, 1 - mine), (kept, mine)):
                part = 2 * y + core
                own = pl.ds(pl.multiple_of(ROWS * part, ROWS), ROWS)
                at = put(out, y, 0, [upper[own, lanes(t)] for t in range(3)])
                for t in range(3):
                    at = put(out, y, at, early_rows(upper_far, part, lanes(t)))
                for t in range(4):
                    at = put(out, y, at, early_rows(lower, part, lanes(t)))
                for t in range(3):
                    at = put(out, y, at, early_rows(lower_far, part, lanes(t)))

    shape = (places, EARLY_ALL, LANES)
    outputs = [(shape, F32), (shape, BF16), ((height, depth), BF16), ((height, depth), BF16)]
    scratch = ((width, EARLY), (EARLY, width), (EARLY, EARLY), (EARLY, EARLY))
    return products(kernel, (near, *start, *half[2:], first, second), outputs, near.size * EARLY, scratch)


def pack_middle(near, ahead0, behind0, ahead1, behind1, first, second):
    width = near.shape[0]
    height, depth = first.shape
    columns = pl.ds(0, depth)
    low, high = pl.ds(0, ahead0.shape[0]), pl.ds(ahead0.shape[0], ahead1.shape[0])

    def kernel(near, ahead0, behind0, ahead1, behind1, first, second, upper, tall, tall_t, corner):
        last, prior = pick(first, second)
        upper[...] = contract(near[:, columns], last)
        tall[low, :] = contract(behind0[:, columns], last)
        tall[high, :] = contract(behind1[...], last)
        tall_t[low, :] = contract(ahead0[:, columns], prior)
        tall_t[high, :] = contract(ahead1[...], prior)
        corner[...] = contract(prior, last)

    outputs = [((rows, height), F32) for rows in (width, EARLY, EARLY, height)]
    inputs = (near, ahead0, behind0, ahead1, behind1, first, second)
    return products(kernel, inputs, outputs, 3 * near.size * height)


def pack_late(near, ahead0, behind0, ahead1, behind1, middle, first, second):
    width = near.shape[0]
    places = PARTS // 2
    depth = first.shape[1]
    columns = pl.ds(near.shape[1] - depth, depth)
    low, high = pl.ds(0, ahead0.shape[0]), pl.ds(ahead0.shape[0], ahead1.shape[0])

    def kernel(near, ahead0, behind0, ahead1, behind1, upper0, tall0, tall_t0, corner0, first, second, kept, sent, upper, lower, tall, wide, tall_t, wide_t):
        last, prior = pick(first, second)
        value = upper0[...] + contract(near[:, columns], last)
        upper[...] = value
        lower[...] = value.T
        tall[low, :] = tall0[low, :] + contract(behind0[:, columns], last)
        tall[high, :] = tall0[high, :] + contract(behind1[...], last)
        wide_t[:, pl.ds(0, EARLY)] = tall[...].T
        tall_t[low, :] = tall_t0[low, :] + contract(ahead0[:, columns], prior)
        tall_t[high, :] = tall_t0[high, :] + contract(ahead1[...], prior)
        wide[:, pl.ds(0, EARLY)] = tall_t[...].T
        value = corner0[...] + contract(prior, last)
        wide[:, pl.ds(EARLY, LATE)] = value
        wide_t[:, pl.ds(EARLY, LATE)] = value.T
        mine = spot()[0]
        for y in range(places):
            for out, core in ((sent, 1 - mine), (kept, mine)):
                part = 2 * y + core
                own = pl.ds(pl.multiple_of(ROWS * part, ROWS), ROWS)
                at = put(out, y, 0, [upper[own, :]])
                at = put(out, y, at, early_rows(tall, part, lanes(0)))
                at = put(out, y, at, [late_rows(wide, part, lanes(t)) for t in range(4)])
                at = put(out, y, at, [late_rows(lower, part, lanes(t)) for t in range(4)])
                at = put(out, y, at, early_rows(tall_t, part, lanes(0)))
                at = put(out, y, at, [late_rows(wide_t, part, lanes(t)) for t in range(4)])

    shape = (places, LATE_ALL, LANES)
    inputs = (near, ahead0, behind0, ahead1, behind1, *middle, first, second)
    scratch = ((width, LATE), (LATE, width), (EARLY, LATE), (LATE, width), (EARLY, LATE), (LATE, width))
    return products(kernel, inputs, [(shape, F32), (shape, BF16)], 3 * near.size * LATE, scratch)


def join_core(kept, received):
    places, rows, width = kept.shape

    def kernel(kept, received, total, *pieces):
        y = spot()[1]
        total[...] = kept[y] + received[y].astype(F32)
        for steps in range(1, places):
            target = lax.rem(y + steps, places)
            pieces[steps - 1][...] = (kept[target] + received[target].astype(F32)).astype(BF16)

    shape = (rows, width)
    return pl.pallas_call(
        kernel,
        in_specs=[VMEM, VMEM],
        out_specs=[VMEM] * places,
        out_shape=[jax.ShapeDtypeStruct(shape, F32)] + [jax.ShapeDtypeStruct(shape, BF16)] * (places - 1),
        compiler_params=params(),
        cost_estimate=cost(kept.size, 8 * kept.size),
    )(kept, received)


def after(value, *others):
    return lax.optimization_barrier((value, *others))[0]


def send_places(pieces):
    received = []
    for steps in (1, 2, 3):
        received.append(shift_y(pieces[steps - 1], steps))
    return received


def gather(refs, span):
    total, *received = refs
    value = total[span, :]
    for piece in received:
        value = value + piece[span, :].astype(F32)
    return value


def write_pair(even, first, second, lower, upper_far):
    def write(low, far):
        low[pl.ds(0, lower.shape[0]), :] = lower
        far[pl.ds(0, upper_far.shape[0]), :] = upper_far
        rest = lower.shape[0] - upper_far.shape[0]
        far[pl.ds(upper_far.shape[0], rest), :] = jnp.zeros((rest, lower.shape[1]), BF16)

    pl.when(even)(lambda: write(first, second))
    pl.when(jnp.logical_not(even))(lambda: write(second, first))


def join_group(total, received, first_rows, second_rows):
    rows, width = total.shape
    height = rows - first_rows - second_rows

    def kernel(total, one, two, three, upper, first, second):
        refs = (total, one, two, three)
        upper[...] = gather(refs, pl.ds(0, first_rows))
        far = gather(refs, pl.ds(first_rows, second_rows)).astype(BF16)
        low = gather(refs, pl.ds(first_rows + second_rows, height)).astype(BF16)
        write_pair(on_even(), first, second, low, far)

    outputs = [((first_rows, width), F32), ((height, width), BF16), ((height, width), BF16)]
    return products(kernel, (total, *received), outputs, 3 * total.size)


def join_late(prior, total, received):
    rows, width = total.shape
    height = rows - LATE_U1 - LATE_U2
    before = prior.shape[0]

    def kernel(prior, total, one, two, three, upper, first, second):
        refs = (total, one, two, three)
        upper[...] = gather(refs, pl.ds(0, LATE_U1))
        far = gather(refs, pl.ds(LATE_U1, LATE_U2)).astype(BF16)
        low = gather(refs, pl.ds(LATE_U1 + LATE_U2, height)).astype(BF16)
        second[pl.ds(0, before), :] = prior[...]
        write_pair(on_even(), first, second.at[pl.ds(before, height), :], low, far)

    outputs = [((LATE_U1, width), F32), ((height, width), BF16), ((before + height, width), BF16)]
    return products(kernel, (prior, total, *received), outputs, 3 * total.size)


def restore(order, early, late):
    width = order.shape[0]

    def kernel(order, early, late, out):
        blocks = [early[pl.ds(ROWS * t, ROWS), :] for t in range(3)] + [late[...]]
        value = jnp.concatenate(blocks, axis=1)
        exact = order[...].astype(F32)
        out[...] = jnp.dot(value, exact, preferred_element_type=F32, precision=lax.Precision.HIGHEST)

    return pl.pallas_call(
        kernel,
        in_specs=[VMEM] * 3,
        out_specs=VMEM,
        out_shape=jax.ShapeDtypeStruct((ROWS, width), F32),
        compiler_params=params(),
        cost_estimate=cost(2 * 6 * ROWS * width**2, 4 * width**2),
    )(order, early, late)


def assemble(order, upper, early, late, second):
    width = order.shape[0]
    before = early.shape[0]

    def rows(early, late, base, late_base):
        body = jnp.concatenate(
            [early[pl.ds(base + 48 * t, 48), :] for t in range(3)] + [late[pl.ds(late_base, 48), :]], axis=1
        )
        last = jnp.concatenate([late[pl.ds(late_base + 48 + 16 * t, 16), :] for t in range(4)], axis=1)
        return jnp.concatenate([body[:16], last, body[16:]], axis=0)

    def kernel(order, upper, early, late, second, out):
        even = on_even()
        out[0, 0] = upper[...]
        tail = second.at[pl.ds(before, late.shape[0]), :]

        def write(far, far_late, low, low_late):
            exact = order[...]
            out[0, 1] = jnp.dot(rows(far, far_late, 0, 0), exact, preferred_element_type=F32)
            for t in range(4):
                out[0, 2, pl.ds(0, 16), lanes(t)] = low[pl.ds(48 * t, 16), :].astype(F32)
                out[0, 2, pl.ds(16, 16), lanes(t)] = low_late[pl.ds(16 * t, 16), :].astype(F32)
                out[0, 2, pl.ds(32, 32), lanes(t)] = low[pl.ds(48 * t + 16, 32), :].astype(F32)
            out[0, 3] = jnp.dot(rows(low, low_late, 192, 64), exact, preferred_element_type=F32)

        pl.when(even)(lambda: write(early, late, second, tail))
        pl.when(jnp.logical_not(even))(lambda: write(second, tail, early, late))

    outputs = [((1, 4, ROWS, width), F32)]
    return products(kernel, (order, upper, early, late, second), outputs, 4 * ROWS * width**2)[0]


def natural_order(width):
    index = jnp.arange(width)
    low = ROWS * (index // 16) + index % 16
    high = ROWS * ((index - 128) // 32) + 32 + index % 32
    last = ROWS * ((index - EARLY) // 16) + 16 + index % 16
    place = jnp.where(index < 128, low, jnp.where(index < EARLY, high, last))
    return (place[:, None] == jnp.arange(width)[None, :]).astype(BF16)


def body(factors, density, screen):
    count, width = factors.shape[1], factors.shape[2]
    owned, blocks = factors[0].reshape(count, PARTS, ROWS, width), density[0]
    first, second = [], []
    source = owned
    for chunk in CHUNKS:
        one, two = split(source, blocks, screen, *chunk)
        source = after(owned, one)
        second.append(swap_atoms(two, 1))
        first.append(swap_atoms(one, 0))
    near = transform(source, blocks, screen)
    start = begin(near, first[:2], second[:2])
    half = advance(near, *start[:2], first[2], second[2])
    kept, sent, ahead, behind = pack_early(near, start, half, first[3], second[3])
    total, *pieces = join_core(kept, swap_core(sent))
    received = send_places(pieces)
    middle = pack_middle(near, *start[:2], *half[:2], first[4], second[4])
    kept, sent = pack_late(near, *start[:2], ahead, behind, middle, first[5], second[5])
    late_total, *late_pieces = join_core(kept, swap_core(sent))
    late_received = send_places(late_pieces)
    upper, early_first, early_second = join_group(after(total, *late_pieces), received, EARLY_U1, EARLY_U2)
    early_first = swap_atoms(early_first, 0)
    late_upper, one, two = join_late(early_second, late_total, late_received)
    two = swap_atoms(two, 1)
    one = swap_atoms(one, 0)
    order = natural_order(width)
    upper = restore(order, upper, late_upper)
    return assemble(order, upper, early_first, one, two)


def solution(mesh):
    in_specs = (P("atoms", "aux", None, None), P("atoms", None, None, None), P("atoms", None))
    out_specs = P("atoms", None, "aux", None)
    return jax.shard_map(body, mesh=mesh, in_specs=in_specs, out_specs=out_specs, check_vma=False)
```
